256 devices in a mesh: rows: 128 (over z, x, y), half: 2 (over core).
Axes of the slice: x: 4, y: 4, z: 8, core: 2. Of those that a mesh axis runs over, the one named last changes fastest.
Arguments:
- source_feats: bfloat16 [131072, 1024], P('rows', 'half'), may hold values from -6 to 6
- rel_weight: bfloat16 [3, 2, 512, 512], P(None, 'half'), may hold values from -0.25 to 0.25
- tiles: bfloat16 [4096, 64, 512], P('rows'), may hold values from -0.25 to 0.25
- src_blk: int32 [4096, 8], P('rows'), may hold values from 0 to 15
- rel_id: int32 [4096, 8], P('rows'), may hold values from 0 to 2
- owner: int32 [4096, 1], P('rows'), may hold values from 0 to 127; in each aligned block of 32 rows (0 to 31, 32 to 63, ...) at most 2 rows name the same one
- local_blk: int32 [4096], P('rows'), may hold values from 0 to 31
- in_degree: int32 [262144], P('rows'), may hold values from 1 to 16
- mix_weight: bfloat16 [1024, 1024], P(None, 'half'), may hold values from -0.1875 to 0.1875
- bias: float32 [1024], P('half'), may hold values from -0.5 to 0.5
Outputs:
- out: bfloat16 [262144, 1024], P('rows', 'half')
The draws below stay inside these ranges and needn't reach their ends.
Inputs may be any that keep to these rules, and one draw needn't show every extreme that they name: Among the 32 rows held by one device along rows, no owner is named more than 2 times, some owner exactly 2 times, and every owner is named somewhere.
All inputs are finite; a program needn't handle non-finite values.
Results may differ from the reference program's by a relative error of at most 0.0054.
Values may be sent and summed in bfloat16 or wider, within the bound.
A program may use at most 128 MiB of HBM per device.

```python
import math
import jax
import jax.numpy as jnp
import numpy as np
from jax import lax

D = 1024
REL = 3
TILE = 64
KT = 8
PB = 32
SRC_DEV = 1024
CAP = 2
LB = 32
OWNERS = 128
SOURCES = 131072
TARGETS = 262144
PARTS_SIZE = 4096
N_ROWS = 128


def plant(result, own_key, low, top_value):
    place = [jax.random.randint(jax.random.fold_in(own_key, axis), (), 0, length) for axis, length in enumerate(result.shape)]
    longest = result.shape.index(max(result.shape))
    beside = place[:longest] + [(place[longest] + 1) % result.shape[longest]] + place[longest + 1:]
    return result.at[tuple(place)].set(low).at[tuple(beside)].set(top_value)


def shard_levels(key, dims, split, least, high):
    def one(dim, shards_of):
        steps = jax.random.uniform(jax.random.fold_in(jax.random.fold_in(key, 6), dim), (shards_of,), jnp.float32, least / len(split), high / len(split))
        return jnp.repeat(jnp.exp(steps), dims[dim] // shards_of).reshape((-1,) + (1,) * (len(dims) - dim - 1))

    loudness = one(*split[0])
    for cut in split[1:]:
        loudness = loudness * one(*cut)
    return loudness


def shared_out(stream_key, own, number, rows, number_of, top, most, slope):
    ranking = jax.random.permutation(stream_key, number_of)
    crowded, ordinary = load_shares(number_of, rows * top, most, slope, True), load_shares(number_of, rows * top, most, slope, False)
    places = jnp.arange(number_of)

    def named(lengths, offset_by):
        used = int((lengths > 0).sum())
        fixed = max(1, used // 4)
        shifted = fixed + (places - fixed + offset_by * (used - fixed)) % max(1, number_of - fixed)
        return jnp.zeros((number_of,), jnp.int32).at[ranking[jnp.where(places < fixed, places, shifted)]].set(jnp.asarray(lengths, jnp.int32))

    lengths = jnp.where(number % 4 == 0, named(crowded, number // 4), named(ordinary, number - number // 4 - 1))
    mixed = jax.random.permutation(jax.random.fold_in(own, 3), number_of)
    giver, taker = mixed[0:number_of // 2 * 2:2], mixed[1:number_of // 2 * 2:2]
    margin = jnp.minimum(lengths[giver] - 1, most - lengths[taker]) // 2
    margin = jnp.where((giver == ranking[0]) | (taker == ranking[0]) | (lengths[taker] == 0), 0, jnp.maximum(margin, 0))
    shifted = jax.random.randint(jax.random.fold_in(own, 4), (number_of // 2,), 0, 1 << 20) % (margin + 1)
    lengths = lengths.at[giver].add(-shifted).at[taker].add(shifted)
    items = jnp.searchsorted(jnp.cumsum(lengths), jnp.arange(rows * top), side="right").astype(jnp.int32)
    grid = items.reshape(top, rows).T
    grid = grid[jax.random.permutation(jax.random.fold_in(own, 1), rows)]
    offset_by = jax.random.randint(jax.random.fold_in(own, 2), (rows, 1), 0, top)
    return jnp.take_along_axis(grid, (jnp.arange(top)[None, :] + offset_by) % top, axis=1)


def load_shares(number_of, total, bound, slope, full):
    weights = [(1 << 20) // math.isqrt(rank ** slope) + 1 for rank in range(1, number_of + 1)]
    largest = bound if full else min(bound, max(-(-total // number_of), total * weights[0] // sum(weights)))
    least = 1 if total - largest >= number_of - 1 else 0
    counts, surplus = [largest] + [least] * (number_of - 1), total - largest - least * (number_of - 1)
    while surplus > 0:
        movable = [i for i in range(1, number_of) if counts[i] < largest] or [i for i in range(1, number_of) if counts[i] < bound]
        whole, left = sum([weights[i] for i in movable]), surplus
        for i in movable:
            addition = min(bound - counts[i], max(1, left * weights[i] // whole), surplus)
            counts[i] = counts[i] + addition
            surplus = surplus - addition
    return np.array(counts)


def scatter_about(own_key, shape, spread, reach, shards=(), held_as=jnp.bfloat16):
    result = jax.random.normal(own_key, shape, jnp.float32) * spread
    if len(shards) > 0:
        result = shard_levels(own_key, shape, shards, -0.22, 0.18) * result
    return jnp.clip(result, min=-reach, max=reach).astype(held_as)


def setup_inputs(seed: int = 0) -> dict:
    keys = jax.random.split(jax.random.key(seed), 11)
    source_feats = scatter_about(keys[0], (SOURCES, D), 1.0, 6.0, ((0, 128), (1, 2)))
    rel_weight = scatter_about(keys[1], (REL, 2, D // 2, D // 2), (D // 2) ** -0.5, 0.25, ((1, 2),))
    tiles = scatter_about(keys[2], (PARTS_SIZE, TILE, KT * TILE), (KT * TILE) ** -0.5, 0.25, ((0, 128),))
    src_blk = plant(jax.random.randint(keys[3], (PARTS_SIZE, KT), 0, SRC_DEV // TILE), jax.random.fold_in(keys[3], 1), 0, (SRC_DEV // TILE) - 1).astype(jnp.int32)
    rel_id = plant(jax.random.randint(keys[4], (PARTS_SIZE, KT), 0, REL), jax.random.fold_in(keys[4], 1), 0, REL - 1).astype(jnp.int32)
    owner_keys = jax.random.split(jax.random.fold_in(keys[5], 1), PARTS_SIZE // PB)
    owner_turns = jax.random.permutation(jax.random.fold_in(keys[5], 3), PARTS_SIZE // PB)
    owner = jax.vmap(lambda own, number: shared_out(jax.random.fold_in(keys[5], 2), own, number, PB, OWNERS, 1, CAP, 2))(owner_keys, owner_turns).reshape((PARTS_SIZE, 1))
    local_blk = plant(jax.random.randint(keys[6], (PARTS_SIZE,), 0, LB), jax.random.fold_in(keys[6], 1), 0, LB - 1).astype(jnp.int32)
    in_degree = plant(jax.random.randint(keys[7], (TARGETS,), 1, 17), jax.random.fold_in(keys[7], 1), 1, 16).astype(jnp.int32)
    mix_weight = scatter_about(keys[8], (D, D), D ** -0.5, 0.1875, ((1, 2),))
    bias = jnp.clip(jax.random.uniform(keys[9], (D,), jnp.float32, -0.5, 0.5) * shard_levels(keys[9], (D,), ((0, 2),), -0.4, 0.0), -0.5, 0.5)
    return {"source_feats": source_feats, "rel_weight": rel_weight, "tiles": tiles, "src_blk": src_blk, "rel_id": rel_id, "owner": owner, "local_blk": local_blk, "in_degree": in_degree, "mix_weight": mix_weight, "bias": bias}


def reference(source_feats, rel_weight, tiles, src_blk, rel_id, owner, local_blk, in_degree, mix_weight, bias):
    half_w = D // 2
    n_src_blocks = SRC_DEV // TILE
    weights = rel_weight.astype(jnp.float32)

    def one_device(total, device):
        feats = lax.dynamic_slice_in_dim(source_feats, device * SRC_DEV, SRC_DEV, 0).astype(jnp.float32)
        lower = jnp.einsum('sj,rjc->rsc', feats[:, :half_w], weights[:, 0])
        upper = jnp.einsum('sj,rjc->rsc', feats[:, half_w:], weights[:, 1])
        msgs = jnp.concatenate([lower, upper], axis=2).astype(jnp.bfloat16)
        blocks = msgs.reshape(REL * n_src_blocks, TILE, D)
        start = (device * PB).astype(jnp.int32)
        mine = lax.dynamic_slice_in_dim(tiles, start, PB, 0).astype(jnp.float32).reshape(PB, TILE, KT, TILE)
        sources = lax.dynamic_slice_in_dim(src_blk, start, PB, 0)
        relations = lax.dynamic_slice_in_dim(rel_id, start, PB, 0)
        targets = lax.dynamic_slice_in_dim(owner, start, PB, 0)[:, 0] * LB + lax.dynamic_slice_in_dim(local_blk, start, PB, 0)
        picked = blocks[(relations * n_src_blocks + sources).astype(jnp.int32)].astype(jnp.float32)
        partial_value = jnp.einsum('pikj,pkjc->pic', mine, picked).astype(jnp.bfloat16)
        total = total.at[targets.astype(jnp.int32)].add(partial_value.astype(jnp.float32))
        return total, None

    start_total = jnp.zeros((TARGETS // TILE, TILE, D), jnp.float32)
    total, _ = lax.scan(one_device, start_total, jnp.arange(N_ROWS, dtype=jnp.int32))
    agg = (total.reshape(TARGETS, D) / in_degree.astype(jnp.float32)[:, None]).astype(jnp.bfloat16)
    mixed = jnp.dot(agg, mix_weight, preferred_element_type=jnp.float32) + bias
    return jax.nn.relu(mixed).astype(jnp.bfloat16)
```

```python
import functools

import jax
import jax.numpy as jnp
from jax import lax
from jax.experimental import pallas as pl
from jax.experimental.pallas import tpu as pltpu
from jax.sharding import PartitionSpec as P

MESH = pl.DeviceIdType.MESH
NZ, NX, NY = 8, 4, 4
ROWS = NZ * NX * NY
TILE = 64
LB = 32

Z_LOCAL, Z_CAP = 12, (24, 20, 14, 6)
X_LOCAL, X_CAP = 40, (40, 20)
MERGE = 144
Y_FAR = LB // 2
Y_LIST = LB + Y_FAR

COLS = 128
HEIGHT = 32
COL_CHUNKS = 4
ROW_CHUNKS = TILE // HEIGHT
CHUNKS = COL_CHUNKS * ROW_CHUNKS


def bases(local, caps, start):
    right, left, at = [], [], start + local
    for cap in caps:
        right.append(at)
        at += cap
    for cap in caps:
        left.append(at)
        at += cap
    return right, left, at


Z_RIGHT, Z_LEFT, Z_SLOTS = bases(Z_LOCAL, Z_CAP, 0)
X_RIGHT, X_LEFT, X_SLOTS = bases(X_LOCAL, X_CAP, 1)


def tri(n):
    return (jnp.arange(n)[:, None] < jnp.arange(n)[None, :]).astype(jnp.bfloat16)


def before(masks):
    shape = masks.shape
    flat = masks.astype(jnp.bfloat16).reshape(-1, shape[-1])
    counts = jnp.dot(flat, tri(shape[-1]), preferred_element_type=jnp.float32)
    return counts.astype(jnp.int32).reshape(shape)


def listed(delta, ring, n_caps, right_base, left_base, local_base):
    half = ring // 2
    tie = delta == half
    odd = before(tie) % 2
    to_right = ((delta >= 1) & (delta < half)) | (tie & (odd == 0))
    to_left = ((delta > half) & (delta < ring)) | (tie & (odd == 1))
    dist = jnp.where(delta <= half, delta, ring - delta)
    masks = [delta == 0]
    masks += [to_right & (dist == k) for k in range(1, half + 1)]
    masks += [to_left & (dist == k) for k in range(1, half + 1)]
    masks = jnp.stack(masks)
    ranks = before(masks)
    totals = jnp.sum(masks.astype(jnp.int32), axis=-1, keepdims=True)
    place = jnp.where(masks[0], ranks[0], 0)
    address = jnp.where(masks[0], local_base + ranks[0], 0)
    for side, base in ((0, right_base), (1, left_base)):
        farther = jnp.zeros_like(totals[0])
        for k in range(half, 0, -1):
            at = 1 + side * half + k - 1
            spot = farther + ranks[at]
            place = jnp.where(masks[at], spot, place)
            address = jnp.where(masks[at], base[k - 1] + spot, address)
            farther = farther + totals[at]
    which = jnp.where(to_right, 1, 0) + jnp.where(to_left, 2, 0)
    return address, which, place


def table(value, valid, which, place, sizes):
    parts = []
    for number, size in enumerate(sizes):
        spot = jnp.arange(size)[:, None]
        hit = (place[None, :] == spot) & ((which == number) & valid)[None, :]
        parts.append(jnp.sum(jnp.where(hit, value[None, :], 0), axis=1))
    return jnp.concatenate(parts).astype(jnp.int32)


def tables(keys, me):
    owner, block = keys // LB, keys % LB
    dz, dx, dy = owner // (NX * NY), (owner // NY) % NX, owner % NY
    number = jnp.arange(ROWS)
    sz, sx, sy = number // (NX * NY), (number // NY) % NX, number % NY
    mz, mx, my = me // (NX * NY), (me // NY) % NX, me % NY

    grid = lambda a: lax.dynamic_index_in_dim(a.reshape(NZ, NX, NY, -1), my, 2, keepdims=False)
    gz, gx, gy, gb = grid(dz), grid(dx), grid(dy), grid(block)
    z_delta = (gz - jnp.arange(NZ)[:, None, None]) % NZ
    z_addr, z_which, z_place = listed(z_delta, NZ, len(Z_CAP), Z_RIGHT, Z_LEFT, 0)
    mine = lambda a: lax.dynamic_index_in_dim(
        lax.dynamic_index_in_dim(a, mz, 0, keepdims=False), mx, 0, keepdims=False
    )
    parts = keys.shape[1]
    z_tab = table(
        jnp.arange(parts), jnp.ones((parts,), bool), mine(z_which), mine(z_place),
        (Z_LOCAL, Z_CAP[0], Z_CAP[0]),
    )

    lines = lambda a: a.transpose(1, 0, 2).reshape(NX, NZ * parts)
    here = lines(gz) == mz
    lx = lines(gx)
    x_delta = jnp.where(here, (lx - jnp.arange(NX)[:, None]) % NX, NX)
    x_addr, x_which, x_place = listed(x_delta, NX, len(X_CAP), X_RIGHT, X_LEFT, 1)
    line = lambda a: lax.dynamic_index_in_dim(a, mx, 0, keepdims=False)
    x_tab = table(
        line(lines(z_addr)), line(here), line(x_which), line(x_place),
        (X_LOCAL, X_CAP[0], X_CAP[0]),
    )

    arrived = (here & (lx == mx)).reshape(-1)
    y_delta = (lines(gy).reshape(-1) - my) % NY
    lb = lines(gb).reshape(-1)
    target = jnp.where(
        y_delta == 0,
        lb,
        jnp.where(
            y_delta == 1,
            LB + Y_FAR + lb,
            jnp.where(
                y_delta == 3,
                LB + Y_LIST + Y_FAR + lb,
                jnp.where(lb < Y_FAR, LB + lb, LB + Y_LIST + lb - Y_FAR),
            ),
        ),
    )
    n_targets = LB + 2 * Y_LIST
    onehot = (target[None, :] == jnp.arange(n_targets)[:, None]) & arrived[None, :]
    hist = jnp.sum(onehot.astype(jnp.int32), axis=1)
    earlier = jnp.arange(n_targets)[None, :] < jnp.arange(n_targets)[:, None]
    start = jnp.sum(jnp.where(earlier, hist[None, :], 0), axis=1)
    rank = before(onehot)
    spot = jnp.sum(jnp.where(onehot, rank + start[:, None], 0), axis=0)
    seat = jnp.arange(MERGE)[:, None]
    address = x_addr.reshape(-1)
    y_src = jnp.sum(
        jnp.where((spot[None, :] == seat) & arrived[None, :], address[None, :], 0), axis=1
    )
    y_first = jnp.sum(
        ((start[None, :] == seat) & (hist > 0)[None, :]).astype(jnp.int32), axis=1
    )
    y_last = jnp.where(hist > 0, start + hist - 1, MERGE)

    def ring_fits(counts, local, caps):
        ring = counts.shape[0]
        half = ring // 2
        tied = counts[half]
        ok = jnp.all(counts[0] <= local)
        for side in (0, 1):
            far = (tied + 1 - side) // 2
            ok &= jnp.all(far <= caps[half - 1])
            for k in range(half - 1, 0, -1):
                far = far + counts[k if side == 0 else ring - k]
                ok &= jnp.all(far <= caps[k - 1])
        return ok

    all_z = (dz - sz[:, None]) % NZ
    z_counts = jnp.stack([jnp.sum((all_z == k).astype(jnp.int32), axis=1) for k in range(NZ)])
    fits = ring_fits(z_counts, Z_LOCAL, Z_CAP)
    holder = (dz * NX * NY + (sx * NY + sy)[:, None]).reshape(1, -1)
    holds = (holder == number[:, None]).astype(jnp.bfloat16)
    goes = (((dx - sx[:, None]) % NX).reshape(1, -1) == jnp.arange(NX)[:, None]).astype(jnp.bfloat16)
    x_counts = lax.dot_general(
        goes, holds, (((1,), (1,)), ((), ())), preferred_element_type=jnp.float32
    ).astype(jnp.int32)
    fits &= ring_fits(x_counts, X_LOCAL, X_CAP)
    by_x = x_counts.reshape(NX, NZ, NX, NY)
    for dest in range(NX):
        total = sum(by_x[(dest - at) % NX, :, at, :] for at in range(NX))
        fits &= jnp.all(total <= MERGE)
    y_tab = jnp.concatenate([y_src, y_first, y_last]).astype(jnp.int32)
    return z_tab, x_tab, y_tab, fits


def partials_kernel(picks, feats, weight, tiles, out, msgs):
    n_rel, per = weight.shape[0], feats.shape[0] // TILE
    step = 256
    for r in range(n_rel):
        for s in range(feats.shape[0] // step):
            m = jnp.dot(
                feats[s * step : (s + 1) * step, :], weight[r], preferred_element_type=jnp.float32
            ).astype(jnp.bfloat16)
            at = r * per + s * (step // TILE)
            msgs[at : at + step // TILE] = m.reshape(step // TILE, TILE, m.shape[1])
    kt = tiles.shape[2] // TILE

    def one(p, carry):
        rhs = jnp.concatenate([msgs[picks[p * kt + k]] for k in range(kt)], axis=0)
        v = jnp.dot(tiles[p], rhs, preferred_element_type=jnp.float32).astype(jnp.bfloat16)
        for i in range(ROW_CHUNKS):
            for j in range(COL_CHUNKS):
                out[i * COL_CHUNKS + j, p] = v[
                    i * HEIGHT : (i + 1) * HEIGHT, j * COLS : (j + 1) * COLS
                ]
        return carry

    lax.fori_loop(0, tiles.shape[0], one, 0)


def schedule():
    unit = 1.41 * 2 / CHUNKS / 2
    rings = {
        "z": [c * unit for c in Z_CAP],
        "x": [c * unit for c in X_CAP],
        "y": [Y_LIST * unit, Y_FAR * unit],
    }
    work = {"z": 1.0, "x": 1.0, "y": 3.5, "f": 1.5, "g": 1.5}
    free = {"z": 0.0, "x": 0.0, "y": 0.0, "h": 0.0}
    now, order = 0.0, []
    ready = {("z", 0, c): 0.0 for c in range(CHUNKS)}
    while ready:
        best = None
        for (kind, k, c), t in ready.items():
            start = max(t, now)
            if kind == "z" and k == 0:
                start = max(start, free["z"] - 2.5)
            rank = (start, 0 if k > 0 else 1, c)
            if best is None or rank < best[0]:
                best = (rank, (kind, k, c), start)
        _, (kind, k, c), start = best
        del ready[(kind, k, c)]
        order.append((kind, k, c))
        now = start + (work[kind] if k == 0 else 0.1)
        if kind in rings:
            sends = rings[kind]
            if k < len(sends):
                free[kind] = max(free[kind], now) + sends[k]
                ready[(kind, k + 1, c)] = free[kind] + 1.8
            if k == len(sends):
                follow = {"z": "x", "x": "y", "y": "f"}[kind]
                ready[(follow, 0, c)] = now
        elif kind == "f":
            free["h"] = max(free["h"], now) + 0.8
            ready[("g", 0, c)] = free["h"] + 1.0
    return order


def route_kernel(order, *refs):
    it = iter(refs)
    z_tab, x_tab, y_tab, part, degree, mix, bias, out = [next(it) for _ in range(8)]
    zs = [next(it) for _ in range(CHUNKS)]
    zb = [next(it) for _ in range(CHUNKS)]
    xs = [next(it) for _ in range(CHUNKS)]
    xb = [next(it) for _ in range(CHUNKS)]
    ys = [next(it) for _ in range(CHUNKS)]
    yr = [next(it) for _ in range(CHUNKS)]
    ag = [next(it) for _ in range(CHUNKS)]
    stage, total = next(it), next(it)
    z_send, z_recv, x_send, x_recv, y_send, y_recv, h_send, h_recv = [next(it) for _ in range(8)]

    me, half = lax.axis_index("rows"), lax.axis_index("half")
    mz, mx, my = me // (NX * NY), (me // NY) % NX, me % NY

    def at(z, x, y):
        return {"rows": (z % NZ) * (NX * NY) + (x % NX) * NY + y % NY}

    zp, zm = at(mz + 1, mx, my), at(mz + NZ - 1, mx, my)
    xp, xm = at(mz, mx + 1, my), at(mz, mx + NX - 1, my)
    yp, ym = at(mz, mx, my + 1), at(mz, mx, my + NY - 1)
    other = {"half": 1 - half}

    barrier = pltpu.get_barrier_semaphore()
    neighbours = (zp, zm, xp, xm, yp, ym, other)
    for device in neighbours:
        pl.semaphore_signal(barrier, inc=1, device_id=device, device_id_type=MESH)
    pl.semaphore_wait(barrier, len(neighbours))

    def gather(dst, base, read, tab, off, n):
        def body(j, carry):
            dst[base + j] = read(tab[off + j])
            return carry

        lax.fori_loop(0, n, body, 0, unroll=4)

    def copy(src, dst, send, recv, device):
        return pltpu.make_async_remote_copy(
            src_ref=src, dst_ref=dst, send_sem=send, recv_sem=recv,
            device_id=device, device_id_type=MESH,
        )

    def z_copies(c, k):
        n = Z_CAP[k]
        result = []
        for side, device, base in ((0, zp, Z_RIGHT), (1, zm, Z_LEFT)):
            if k == 0:
                src = zs[c].at[pl.ds(side * n, n)]
            else:
                src = zb[c].at[pl.ds(base[k - 1], n)]
            dst = zb[c].at[pl.ds(base[k], n)]
            result.append(copy(src, dst, z_send.at[c, k, side], z_recv.at[c, k, side], device))
        return result

    def x_copies(c, k):
        n = X_CAP[k]
        result = []
        for side, device, base in ((0, xp, X_RIGHT), (1, xm, X_LEFT)):
            if k == 0:
                src = xs[c].at[pl.ds(side * n, n)]
            else:
                src = xb[c].at[pl.ds(base[k - 1], n)]
            dst = xb[c].at[pl.ds(base[k], n)]
            result.append(copy(src, dst, x_send.at[c, k, side], x_recv.at[c, k, side], device))
        return result

    def y_copies(c, k):
        result = []
        for side, device in ((0, yp), (1, ym)):
            if k == 0:
                src = ys[c].at[pl.ds(LB + side * Y_LIST, Y_LIST)]
                dst = yr[c].at[pl.ds(side * Y_LIST, Y_LIST)]
            else:
                src = yr[c].at[pl.ds(side * Y_LIST, Y_FAR)]
                dst = yr[c].at[pl.ds(2 * Y_LIST + side * Y_FAR, Y_FAR)]
            result.append(copy(src, dst, y_send.at[c, k, side], y_recv.at[c, k, side], device))
        return result

    def h_copy(c):
        return copy(ag[c].at[half], ag[c].at[half], h_send.at[c], h_recv.at[c], other)

    stage[MERGE] = jnp.zeros(stage.shape[1:], stage.dtype)
    for c in range(CHUNKS):
        xb[c][0] = jnp.zeros(xb[c].shape[1:], xb[c].dtype)

    ring = {"z": (z_copies, len(Z_CAP)), "x": (x_copies, len(X_CAP)), "y": (y_copies, 2)}

    for kind, k, c in order:
        row, col = c // COL_CHUNKS, c % COL_CHUNKS
        if kind in ring and k > 0:
            copies, hops = ring[kind]
            for item in copies(c, k - 1):
                item.wait_recv()
            if k < hops:
                for item in copies(c, k):
                    item.start()
        elif kind == "z":
            read = lambda i: part[c, i]
            gather(zs[c], 0, read, z_tab, Z_LOCAL, 2 * Z_CAP[0])
            for item in z_copies(c, 0):
                item.start()
            gather(zb[c], 0, read, z_tab, 0, Z_LOCAL)
        elif kind == "x":
            read = lambda i: zb[c][i]
            gather(xs[c], 0, read, x_tab, X_LOCAL, 2 * X_CAP[0])
            for item in x_copies(c, 0):
                item.start()
            gather(xb[c], 1, read, x_tab, 0, X_LOCAL)
        elif kind == "y":

            def add(j, total_now):
                v = xb[c][y_tab[j]].astype(jnp.float32)
                total_now = jnp.where(y_tab[MERGE + j] > 0, v, total_now + v)
                stage[j] = total_now.astype(stage.dtype)
                return total_now

            lax.fori_loop(0, MERGE, add, jnp.zeros((HEIGHT, COLS), jnp.float32), unroll=4)
            read = lambda i: stage[i]
            gather(ys[c], LB, read, y_tab, 2 * MERGE + LB, 2 * Y_LIST)
            for item in y_copies(c, 0):
                item.start()
            gather(ys[c], 0, read, y_tab, 2 * MERGE, LB)
        elif kind == "f":

            def finish(b, carry):
                v = ys[c][b].astype(jnp.float32) + yr[c][Y_FAR + b].astype(jnp.float32)
                v = v + yr[c][Y_LIST + Y_FAR + b].astype(jnp.float32)
                v = v + yr[c][2 * Y_LIST + b].astype(jnp.float32)
                v = v / degree[b, row * HEIGHT : (row + 1) * HEIGHT, :]
                ag[c][half, b] = v.astype(jnp.bfloat16)
                return carry

            lax.fori_loop(0, LB, finish, 0, unroll=2)
            h_copy(c).start()
        else:
            h_copy(c).wait_recv()
            some = 8
            width = mix.shape[0] // 2
            w = jnp.concatenate(
                [
                    mix[col * COLS : (col + 1) * COLS, :],
                    mix[width + col * COLS : width + (col + 1) * COLS, :],
                ],
                axis=0,
            )

            def mixing(b, carry):
                blocks = pl.ds(b * some, some)
                a = jnp.concatenate(
                    [
                        ag[c][0, blocks].reshape(some * HEIGHT, COLS),
                        ag[c][1, blocks].reshape(some * HEIGHT, COLS),
                    ],
                    axis=1,
                )
                v = jnp.dot(a, w, preferred_element_type=jnp.float32)
                v = v.reshape(some, HEIGHT, v.shape[1])
                if col > 0:
                    v = v + total[blocks]
                if col < COL_CHUNKS - 1:
                    total[blocks] = v
                else:
                    v = jnp.maximum(v + bias[...][None], 0.0)
                    out[blocks, row * HEIGHT : (row + 1) * HEIGHT, :] = v.astype(out.dtype)
                return carry

            lax.fori_loop(0, LB // some, mixing, 0)

    for c in range(CHUNKS):
        for copies, hops in ring.values():
            for k in range(hops):
                for item in copies(c, k):
                    item.wait_send()
        h_copy(c).wait_send()


def vmem():
    return pl.BlockSpec(memory_space=pltpu.VMEM)


def smem():
    return pl.BlockSpec(memory_space=pltpu.SMEM)


def local(
    source_feats, rel_weight, tiles, src_blk, rel_id, owner, local_blk, in_degree, mix_weight, bias
):
    n_rows = lax.axis_size("rows")
    src_dev, half_w = source_feats.shape
    tile = tiles.shape[1]
    parts, per_row = src_blk.shape
    n_rel = rel_weight.shape[0]
    n_src_blocks = src_dev // tile
    n_local = in_degree.shape[0] // tile

    keys = lax.all_gather(owner[:, 0] * LB + local_blk, "rows", axis=0, tiled=False)
    picks = (rel_id * n_src_blocks + src_blk).reshape(-1)
    part = pl.pallas_call(
        partials_kernel,
        out_shape=jax.ShapeDtypeStruct((CHUNKS, parts, HEIGHT, COLS), jnp.bfloat16),
        in_specs=[smem(), vmem(), vmem(), vmem()],
        out_specs=vmem(),
        scratch_shapes=[pltpu.VMEM((n_rel * n_src_blocks, tile, half_w), jnp.bfloat16)],
        cost_estimate=pl.CostEstimate(
            flops=2 * half_w * half_w * (src_dev * n_rel + parts * tile),
            bytes_accessed=7 << 20,
            transcendentals=0,
        ),
    )(picks, source_feats, rel_weight[:, 0], tiles)
    z_tab, x_tab, y_tab, fits = tables(keys, lax.axis_index("rows"))
    degree = in_degree.astype(jnp.float32)

    def routed(part):
        wide = jnp.broadcast_to(degree[:, None], (degree.shape[0], COLS)).reshape(n_local, tile, COLS)
        block = lambda n: [pltpu.VMEM((n, HEIGHT, COLS), jnp.bfloat16)] * CHUNKS
        dma = pltpu.SemaphoreType.DMA
        out = pl.pallas_call(
            functools.partial(route_kernel, schedule()),
            out_shape=jax.ShapeDtypeStruct((n_local, tile, half_w), jnp.bfloat16),
            in_specs=[smem(), smem(), smem()] + [vmem()] * 4,
            out_specs=vmem(),
            scratch_shapes=block(2 * Z_CAP[0])
            + block(Z_SLOTS)
            + block(2 * X_CAP[0])
            + block(X_SLOTS)
            + block(LB + 2 * Y_LIST)
            + block(2 * Y_LIST + 2 * Y_FAR)
            + [pltpu.VMEM((2, n_local, HEIGHT, COLS), jnp.bfloat16)] * CHUNKS
            + [
                pltpu.VMEM((MERGE + 1, HEIGHT, COLS), jnp.bfloat16),
                pltpu.VMEM((n_local, HEIGHT, half_w), jnp.float32),
                dma((CHUNKS, len(Z_CAP), 2)),
                dma((CHUNKS, len(Z_CAP), 2)),
                dma((CHUNKS, len(X_CAP), 2)),
                dma((CHUNKS, len(X_CAP), 2)),
                dma((CHUNKS, 2, 2)),
                dma((CHUNKS, 2, 2)),
                dma((CHUNKS,)),
                dma((CHUNKS,)),
            ],
            compiler_params=pltpu.CompilerParams(
                collective_id=0, has_side_effects=True, vmem_limit_bytes=64 * 1024 * 1000
            ),
        )(z_tab, x_tab, y_tab, part, wide, mix_weight, bias[None, :])
        return out.reshape(n_local * tile, half_w)

    def dense(part):
        capacity = max(2, 2 * parts // n_rows)
        partials = part.reshape(ROW_CHUNKS, COL_CHUNKS, parts, HEIGHT, COLS)
        partials = partials.transpose(2, 0, 3, 1, 4).reshape(parts, tile * half_w)
        target_dev = owner[:, 0]
        positions = jnp.arange(parts, dtype=jnp.int32)
        earlier = (target_dev[:, None] == target_dev[None, :]) & (
            positions[None, :] < positions[:, None]
        )
        rank = jnp.sum(earlier.astype(jnp.int32), axis=1)
        slot = target_dev * capacity + rank
        slot_ids = jnp.arange(n_rows * capacity, dtype=jnp.int32)
        placing = slot_ids[:, None] == slot[None, :]
        outgoing = jnp.dot(
            placing.astype(jnp.bfloat16), partials, preferred_element_type=jnp.float32
        ).astype(jnp.bfloat16)
        out_ids = jnp.sum(jnp.where(placing, local_blk[None, :] + 1, 0), axis=1) - 1
        block_index = jnp.arange(n_local, dtype=jnp.int32)
        arrived = lax.all_to_all(outgoing, "rows", split_axis=0, concat_axis=0, tiled=True)
        arrived_ids = lax.all_to_all(out_ids, "rows", split_axis=0, concat_axis=0, tiled=True)
        selector = (arrived_ids[None, :] == block_index[:, None]).astype(jnp.bfloat16)
        summed = jnp.dot(selector, arrived, preferred_element_type=jnp.float32)
        summed = summed.reshape(n_local * tile, half_w)
        agg = (summed / degree[:, None]).astype(jnp.bfloat16)
        theirs = lax.ppermute(agg, "half", [(0, 1), (1, 0)])
        half = lax.axis_index("half")
        w_mine = lax.dynamic_slice_in_dim(mix_weight, half * half_w, half_w, 0)
        w_theirs = lax.dynamic_slice_in_dim(mix_weight, (1 - half) * half_w, half_w, 0)
        mixed = jnp.dot(
            jnp.concatenate([agg, theirs], axis=1),
            jnp.concatenate([w_mine, w_theirs], axis=0),
            preferred_element_type=jnp.float32,
        )
        return jax.nn.relu(mixed + bias).astype(jnp.bfloat16)

    return lax.cond(fits, routed, dense, part)


def solution(mesh):
    placed = (
        P("rows", "half"),
        P(None, "half", None, None),
        P("rows", None, None),
        P("rows", None),
        P("rows", None),
        P("rows", None),
        P("rows"),
        P("rows"),
        P(None, "half"),
        P("half"),
    )
    return jax.shard_map(
        local, mesh=mesh, in_specs=placed, out_specs=P("rows", "half"), check_vma=False
    )
```

```python
import functools

import jax
import jax.numpy as jnp
from jax import lax
from jax.experimental import pallas as pl
from jax.experimental.pallas import tpu as pltpu
from jax.sharding import PartitionSpec as P

MESH = pl.DeviceIdType.MESH
NZ, NX, NY = 8, 4, 4
ROWS = NZ * NX * NY
TILE = 64
LB = 32

Z_LOCAL, Z_CAP = 12, (24, 20, 14, 6)
X_LOCAL, X_CAP = 30, (32, 14)
MERGE = 96
Y_CAP = (24, 11)
GROUP = LB // NX
FAR = GROUP // 2
R_LIST = GROUP + FAR

COLS = 128
HEIGHT = 32
COL_CHUNKS = 4
ROW_CHUNKS = TILE // HEIGHT
CHUNKS = COL_CHUNKS * ROW_CHUNKS


def bases(local, caps, start):
    right, left, at = [], [], start + local
    for cap in caps:
        right.append(at)
        at += cap
    for cap in caps:
        left.append(at)
        at += cap
    return right, left, at


Z_RIGHT, Z_LEFT, Z_SLOTS = bases(Z_LOCAL, Z_CAP, 0)
X_RIGHT, X_LEFT, X_SLOTS = bases(X_LOCAL, X_CAP, 1)
Y_RIGHT, Y_LEFT, Y_SLOTS = bases(LB, Y_CAP, 1)


def tri(n):
    return (jnp.arange(n)[:, None] < jnp.arange(n)[None, :]).astype(jnp.bfloat16)


def before(masks):
    shape = masks.shape
    flat = masks.astype(jnp.bfloat16).reshape(-1, shape[-1])
    counts = jnp.dot(flat, tri(shape[-1]), preferred_element_type=jnp.float32)
    return counts.astype(jnp.int32).reshape(shape)


def listed(delta, ring, n_caps, right_base, left_base, local_base):
    half = ring // 2
    tie = delta == half
    odd = before(tie) % 2
    to_right = ((delta >= 1) & (delta < half)) | (tie & (odd == 0))
    to_left = ((delta > half) & (delta < ring)) | (tie & (odd == 1))
    dist = jnp.where(delta <= half, delta, ring - delta)
    masks = [delta == 0]
    masks += [to_right & (dist == k) for k in range(1, half + 1)]
    masks += [to_left & (dist == k) for k in range(1, half + 1)]
    masks = jnp.stack(masks)
    ranks = before(masks)
    totals = jnp.sum(masks.astype(jnp.int32), axis=-1, keepdims=True)
    place = jnp.where(masks[0], ranks[0], 0)
    address = jnp.where(masks[0], local_base + ranks[0], 0)
    for side, base in ((0, right_base), (1, left_base)):
        farther = jnp.zeros_like(totals[0])
        for k in range(half, 0, -1):
            at = 1 + side * half + k - 1
            spot = farther + ranks[at]
            place = jnp.where(masks[at], spot, place)
            address = jnp.where(masks[at], base[k - 1] + spot, address)
            farther = farther + totals[at]
    which = jnp.where(to_right, 1, 0) + jnp.where(to_left, 2, 0)
    return address, which, place


def table(value, valid, which, place, sizes):
    parts = []
    for number, size in enumerate(sizes):
        spot = jnp.arange(size)[:, None]
        hit = (place[None, :] == spot) & ((which == number) & valid)[None, :]
        parts.append(jnp.sum(jnp.where(hit, value[None, :], 0), axis=1))
    return jnp.concatenate(parts).astype(jnp.int32)


def tables(keys, me):
    owner, block = keys // LB, keys % LB
    dz, dx, dy = owner // (NX * NY), (owner // NY) % NX, owner % NY
    number = jnp.arange(ROWS)
    sz, sx, sy = number // (NX * NY), (number // NY) % NX, number % NY
    mz, mx, my = me // (NX * NY), (me // NY) % NX, me % NY

    home, spare = block // GROUP, dx * GROUP + block % GROUP
    grid = lambda a: lax.dynamic_index_in_dim(a.reshape(NZ, NX, NY, -1), my, 2, keepdims=False)
    gz, gx, gy, gb = grid(dz), grid(home), grid(dy), grid(spare)
    z_delta = (gz - jnp.arange(NZ)[:, None, None]) % NZ
    z_addr, z_which, z_place = listed(z_delta, NZ, len(Z_CAP), Z_RIGHT, Z_LEFT, 0)
    mine = lambda a: lax.dynamic_index_in_dim(
        lax.dynamic_index_in_dim(a, mz, 0, keepdims=False), mx, 0, keepdims=False
    )
    parts = keys.shape[1]
    z_tab = table(
        jnp.arange(parts), jnp.ones((parts,), bool), mine(z_which), mine(z_place),
        (Z_LOCAL, Z_CAP[0], Z_CAP[0]),
    )

    lines = lambda a: a.transpose(1, 0, 2).reshape(NX, NZ * parts)
    here = lines(gz) == mz
    lx = lines(gx)
    x_delta = jnp.where(here, (lx - jnp.arange(NX)[:, None]) % NX, NX)
    x_addr, x_which, x_place = listed(x_delta, NX, len(X_CAP), X_RIGHT, X_LEFT, 1)
    line = lambda a: lax.dynamic_index_in_dim(a, mx, 0, keepdims=False)
    x_tab = table(
        line(lines(z_addr)), line(here), line(x_which), line(x_place),
        (X_LOCAL, X_CAP[0], X_CAP[0]),
    )

    holder = (dz * (NX * NY) + home * NY + sy[:, None]).reshape(1, -1)
    wanted = (((dy - sy[:, None]) % NY) * LB + spare).reshape(1, -1)
    n_targets = NY * LB
    holds = (holder == number[:, None]).astype(jnp.bfloat16)
    wants = (wanted == jnp.arange(n_targets)[:, None]).astype(jnp.bfloat16)
    contract = (((1,), (1,)), ((), ()))
    hists = lax.dot_general(holds, wants, contract, preferred_element_type=jnp.float32)
    hists = hists.astype(jnp.int32)
    line_hists = lax.dynamic_slice_in_dim(hists, mz * (NX * NY) + mx * NY, NY, 0)
    hist = lax.dynamic_index_in_dim(line_hists, my, 0, keepdims=False)
    y_delta = jnp.where(line_hists > 0, (jnp.arange(n_targets) // LB)[None, :], NY)
    y_addr, y_which, y_place = listed(y_delta, NY, len(Y_CAP), Y_RIGHT, Y_LEFT, 1)
    seen = lambda a: lax.dynamic_index_in_dim(a, my, 0, keepdims=False)
    start = jnp.sum(jnp.where(tri(n_targets).T > 0, hist[None, :], 0), axis=1)
    last = jnp.where(hist > 0, start + hist - 1, MERGE)
    y_lists = table(last, hist > 0, seen(y_which), seen(y_place), (0, Y_CAP[0], Y_CAP[0]))

    arrived = (here & (lx == mx)).reshape(-1)
    target = ((lines(gy).reshape(-1) - my) % NY) * LB + lines(gb).reshape(-1)
    onehot = (target[None, :] == jnp.arange(n_targets)[:, None]) & arrived[None, :]
    rank = before(onehot)
    spot = jnp.sum(jnp.where(onehot, rank + start[:, None], 0), axis=0)
    seat = jnp.arange(MERGE)[:, None]
    address = x_addr.reshape(-1)
    y_src = jnp.sum(
        jnp.where((spot[None, :] == seat) & arrived[None, :], address[None, :], 0), axis=1
    )
    y_first = jnp.sum(
        ((start[None, :] == seat) & (hist > 0)[None, :]).astype(jnp.int32), axis=1
    )
    finals = []
    for hop in range(1, NY):
        source = (my + NY - hop) % NY
        there = lax.dynamic_index_in_dim(y_addr, source, 0, keepdims=False)
        count = lax.dynamic_index_in_dim(line_hists, source, 0, keepdims=False)
        span = slice(hop * LB, (hop + 1) * LB)
        finals.append(jnp.where(count[span] > 0, there[span], 0))

    def ring_fits(counts, local, caps):
        ring = counts.shape[0]
        half = ring // 2
        tied = counts[half]
        ok = jnp.all(counts[0] <= local)
        for side in (0, 1):
            far = (tied + 1 - side) // 2
            ok &= jnp.all(far <= caps[half - 1])
            for k in range(half - 1, 0, -1):
                far = far + counts[k if side == 0 else ring - k]
                ok &= jnp.all(far <= caps[k - 1])
        return ok

    all_z = (dz - sz[:, None]) % NZ
    z_counts = jnp.stack([jnp.sum((all_z == k).astype(jnp.int32), axis=1) for k in range(NZ)])
    fits = ring_fits(z_counts, Z_LOCAL, Z_CAP)
    keeper = (dz * (NX * NY) + (sx * NY + sy)[:, None]).reshape(1, -1)
    keeps = (keeper == number[:, None]).astype(jnp.bfloat16)
    goes = (((home - sx[:, None]) % NX).reshape(1, -1) == jnp.arange(NX)[:, None]).astype(jnp.bfloat16)
    x_counts = lax.dot_general(goes, keeps, contract, preferred_element_type=jnp.float32)
    fits &= ring_fits(x_counts.astype(jnp.int32), X_LOCAL, X_CAP)
    fits &= jnp.all(jnp.sum(hists, axis=1) <= MERGE)
    y_counts = jnp.sum((hists > 0).astype(jnp.int32).reshape(ROWS, NY, LB), axis=2).T
    fits &= ring_fits(y_counts, LB, Y_CAP)
    y_tab = jnp.concatenate([y_src, y_first, last[:LB], y_lists] + finals).astype(jnp.int32)
    return z_tab, x_tab, y_tab, fits


def partials_kernel(picks, key, feats, weight, tiles, out, keys, msgs, send, recv):
    me = lax.axis_index("rows")
    mz, mx, my = me // (NX * NY), (me // NY) % NX, me % NY

    def at(z, x, y):
        return {"rows": (z % NZ) * (NX * NY) + (x % NX) * NY + y % NY}

    hops = [at(mz + k, mx, my) for k in range(1, NZ)]
    hops += [at(mz, mx + k, my) for k in range(1, NX)]
    hops += [at(mz, mx, my + k) for k in range(1, NY)]
    barrier = pltpu.get_barrier_semaphore()
    for device in hops:
        pl.semaphore_signal(barrier, inc=1, device_id=device, device_id_type=MESH)

    def copies(first, n, src, dst):
        return [
            pltpu.make_async_remote_copy(
                src_ref=src, dst_ref=dst, send_sem=send.at[i], recv_sem=recv.at[i],
                device_id=hops[i], device_id_type=MESH,
            )
            for i in range(first, first + n)
        ]

    along_z = copies(0, NZ - 1, key, keys.at[my, mx, mz])
    along_x = copies(NZ - 1, NX - 1, keys.at[my, mx], keys.at[my, mx])
    along_y = copies(NZ + NX - 2, NY - 1, keys.at[my], keys.at[my])

    def begin(items):
        for item in items:
            item.start()

    def landed(items):
        for item in items:
            item.wait_recv()

    keys[my, mx, mz] = key[...]
    n_rel, per = weight.shape[0], feats.shape[0] // TILE
    step = 256

    def messages(r):
        for s in range(feats.shape[0] // step):
            m = jnp.dot(
                feats[s * step : (s + 1) * step, :], weight[r], preferred_element_type=jnp.float32
            ).astype(jnp.bfloat16)
            spot = r * per + s * (step // TILE)
            msgs[spot : spot + step // TILE] = m.reshape(step // TILE, TILE, m.shape[1])

    kt = tiles.shape[2] // TILE

    def one(p, carry):
        rhs = jnp.concatenate([msgs[picks[p * kt + k]] for k in range(kt)], axis=0)
        v = jnp.dot(tiles[p], rhs, preferred_element_type=jnp.float32).astype(jnp.bfloat16)
        for i in range(ROW_CHUNKS):
            for j in range(COL_CHUNKS):
                out[i * COL_CHUNKS + j, p] = v[
                    i * HEIGHT : (i + 1) * HEIGHT, j * COLS : (j + 1) * COLS
                ]
        return carry

    parts = tiles.shape[0]
    messages(0)
    pl.semaphore_wait(barrier, len(hops))
    begin(along_z)
    for r in range(1, n_rel):
        messages(r)
    lax.fori_loop(0, parts // 4, one, 0)
    landed(along_z)
    begin(along_x)
    lax.fori_loop(parts // 4, 5 * parts // 8, one, 0)
    landed(along_x)
    begin(along_y)
    lax.fori_loop(5 * parts // 8, parts, one, 0)
    landed(along_y)
    for item in along_z + along_x + along_y:
        item.wait_send()


def schedule():
    unit = 1.58 / CHUNKS
    links = {"z": "z", "x": "x", "y": "y", "r": "x"}
    sends = {
        "z": [c * unit for c in Z_CAP],
        "x": [c * unit for c in X_CAP],
        "y": [c * unit for c in Y_CAP],
        "r": [R_LIST * unit, FAR * unit],
    }
    stages = ["z", "x", "y", "r", "g"]
    work = {"z": 0.5, "x": 0.5, "y": 1.2, "r": 0.7, "g": 1.2}
    free = {"z": 0.0, "x": 0.0, "y": 0.0, "h": 0.0}
    now, order = 0.0, []
    ready = {("z", 0, c): 0.0 for c in range(CHUNKS)}
    while ready:
        best = None
        for (kind, k, c), t in ready.items():
            start = max(t, now)
            if kind == "z" and k == 0:
                start = max(start, free["z"] - 2.5)
            rank = (start, 0 if k > 0 else 1, c, -stages.index(kind))
            if best is None or rank < best[0]:
                best = (rank, (kind, k, c), start)
        _, (kind, k, c), start = best
        del ready[(kind, k, c)]
        order.append((kind, k, c))
        now = start + (work[kind] if k == 0 else 0.1)
        if kind == "g":
            continue
        if k < len(sends[kind]):
            link = links[kind]
            free[link] = max(free[link], now) + sends[kind][k]
            ready[(kind, k + 1, c)] = free[link] + 1.8
        elif kind == "r":
            now += 0.7
            free["h"] = max(free["h"], now) + 0.8
            ready[("g", 0, c)] = free["h"] + 1.0
        else:
            ready[(stages[stages.index(kind) + 1], 0, c)] = now
    return order


def route_kernel(order, *refs):
    it = iter(refs)
    z_tab, x_tab, y_tab, part, degree, mix, bias, out = [next(it) for _ in range(8)]
    zs = [next(it) for _ in range(CHUNKS)]
    zb = [next(it) for _ in range(CHUNKS)]
    xs = [next(it) for _ in range(CHUNKS)]
    xb = [next(it) for _ in range(CHUNKS)]
    ys = [next(it) for _ in range(CHUNKS)]
    yb = [next(it) for _ in range(CHUNKS)]
    rs = [next(it) for _ in range(CHUNKS)]
    rb = [next(it) for _ in range(CHUNKS)]
    ag = [next(it) for _ in range(CHUNKS)]
    stage, total = next(it), next(it)
    z_sems, x_sems, y_sems, r_sems = [(next(it), next(it)) for _ in range(4)]
    h_send, h_recv = next(it), next(it)

    me, half = lax.axis_index("rows"), lax.axis_index("half")
    mz, mx, my = me // (NX * NY), (me // NY) % NX, me % NY

    def at(z, x, y):
        return {"rows": (z % NZ) * (NX * NY) + (x % NX) * NY + y % NY}

    zp, zm = at(mz + 1, mx, my), at(mz + NZ - 1, mx, my)
    xp, xm = at(mz, mx + 1, my), at(mz, mx + NX - 1, my)
    yp, ym = at(mz, mx, my + 1), at(mz, mx, my + NY - 1)
    other = {"half": 1 - half}

    barrier = pltpu.get_barrier_semaphore()
    neighbours = (zp, zm, xp, xm, yp, ym, other)
    for device in neighbours:
        pl.semaphore_signal(barrier, inc=1, device_id=device, device_id_type=MESH)
    pl.semaphore_wait(barrier, len(neighbours))

    def gather(dst, base, read, tab, off, n):
        def body(j, carry):
            dst[base + j] = read(tab[off + j])
            return carry

        lax.fori_loop(0, n, body, 0, unroll=4)

    def copy(src, dst, send, recv, device):
        return pltpu.make_async_remote_copy(
            src_ref=src, dst_ref=dst, send_sem=send, recv_sem=recv,
            device_id=device, device_id_type=MESH,
        )

    def hop_copies(sent, held, sems, forward, backward, caps, right, left):
        def copies(c, k):
            n = caps[k]
            result = []
            for side, device, base in ((0, forward, right), (1, backward, left)):
                if k == 0:
                    src = sent[c].at[pl.ds(side * n, n)]
                else:
                    src = held[c].at[pl.ds(base[k - 1], n)]
                dst = held[c].at[pl.ds(base[k], n)]
                result.append(copy(src, dst, sems[0].at[c, k, side], sems[1].at[c, k, side], device))
            return result

        return copies, len(caps)

    def h_copy(c):
        return copy(ag[c].at[half], ag[c].at[half], h_send.at[c], h_recv.at[c], other)

    stage[MERGE] = jnp.zeros(stage.shape[1:], stage.dtype)
    for c in range(CHUNKS):
        xb[c][0] = jnp.zeros(xb[c].shape[1:], xb[c].dtype)
        yb[c][0] = jnp.zeros(yb[c].shape[1:], yb[c].dtype)

    ring = {
        "z": hop_copies(zs, zb, z_sems, zp, zm, Z_CAP, Z_RIGHT, Z_LEFT),
        "x": hop_copies(xs, xb, x_sems, xp, xm, X_CAP, X_RIGHT, X_LEFT),
        "y": hop_copies(ys, yb, y_sems, yp, ym, Y_CAP, Y_RIGHT, Y_LEFT),
        "r": hop_copies(rs, rb, r_sems, xp, xm, (R_LIST, FAR), (0, 2 * R_LIST), (R_LIST, 2 * R_LIST + FAR)),
    }
    y_at = [2 * MERGE, 2 * MERGE + LB, 2 * MERGE + LB + 2 * Y_CAP[0]]

    for kind, k, c in order:
        row, col = c // COL_CHUNKS, c % COL_CHUNKS
        if kind in ring and k > 0:
            copies, hops = ring[kind]
            for item in copies(c, k - 1):
                item.wait_recv()
            if k < hops:
                for item in copies(c, k):
                    item.start()
            elif kind == "r":

                def finish(base, first, n):
                    def body(i, carry):
                        b = first + i
                        v = rb[c][base + i].astype(jnp.float32)
                        v = v / degree[b, row * HEIGHT : (row + 1) * HEIGHT, :]
                        ag[c][half, b] = v.astype(jnp.bfloat16)
                        return carry

                    lax.fori_loop(0, n, body, 0, unroll=4)

                far = 2 * R_LIST
                finish(far + 2 * FAR, mx * GROUP, GROUP)
                finish(FAR, (mx + NX - 1) % NX * GROUP, GROUP)
                finish(R_LIST + FAR, (mx + 1) % NX * GROUP, GROUP)
                finish(far, (mx + 2) % NX * GROUP, GROUP)
                h_copy(c).start()
        elif kind == "z":
            read = lambda i: part[c, i]
            gather(zs[c], 0, read, z_tab, Z_LOCAL, 2 * Z_CAP[0])
            for item in ring["z"][0](c, 0):
                item.start()
            gather(zb[c], 0, read, z_tab, 0, Z_LOCAL)
        elif kind == "x":
            read = lambda i: zb[c][i]
            gather(xs[c], 0, read, x_tab, X_LOCAL, 2 * X_CAP[0])
            for item in ring["x"][0](c, 0):
                item.start()
            gather(xb[c], 1, read, x_tab, 0, X_LOCAL)
        elif kind == "y":

            def add(j, total_now):
                v = xb[c][y_tab[j]].astype(jnp.float32)
                total_now = jnp.where(y_tab[MERGE + j] > 0, v, total_now + v)
                stage[j] = total_now.astype(stage.dtype)
                return total_now

            lax.fori_loop(0, MERGE, add, jnp.zeros((HEIGHT, COLS), jnp.float32), unroll=4)
            read = lambda i: stage[i]
            gather(ys[c], 0, read, y_tab, y_at[1], 2 * Y_CAP[0])
            for item in ring["y"][0](c, 0):
                item.start()
            gather(yb[c], 1, read, y_tab, y_at[0], LB)
        elif kind == "r":

            def collect(dst, base, hop, first, n):
                group = (mx + hop) % NX * GROUP + first

                def body(i, carry):
                    q = group + i
                    v = yb[c][1 + q].astype(jnp.float32)
                    for other_y in range(NY - 1):
                        v = v + yb[c][y_tab[y_at[2] + other_y * LB + q]].astype(jnp.float32)
                    dst[base + i] = v.astype(dst.dtype)
                    return carry

                lax.fori_loop(0, n, body, 0, unroll=4)

            collect(rs[c], 0, 2, 0, FAR)
            collect(rs[c], FAR, 1, 0, GROUP)
            collect(rs[c], R_LIST, 2, FAR, FAR)
            collect(rs[c], R_LIST + FAR, NX - 1, 0, GROUP)
            for item in ring["r"][0](c, 0):
                item.start()
            collect(rb[c], 2 * R_LIST + 2 * FAR, 0, 0, GROUP)
        else:
            h_copy(c).wait_recv()
            some = 8
            width = mix.shape[0] // 2
            w = jnp.concatenate(
                [
                    mix[col * COLS : (col + 1) * COLS, :],
                    mix[width + col * COLS : width + (col + 1) * COLS, :],
                ],
                axis=0,
            )

            def mixing(b, carry):
                blocks = pl.ds(b * some, some)
                a = jnp.concatenate(
                    [
                        ag[c][0, blocks].reshape(some * HEIGHT, COLS),
                        ag[c][1, blocks].reshape(some * HEIGHT, COLS),
                    ],
                    axis=1,
                )
                v = jnp.dot(a, w, preferred_element_type=jnp.float32)
                v = v.reshape(some, HEIGHT, v.shape[1])
                if col > 0:
                    v = v + total[blocks]
                if col < COL_CHUNKS - 1:
                    total[blocks] = v
                else:
                    v = jnp.maximum(v + bias[...][None], 0.0)
                    out[blocks, row * HEIGHT : (row + 1) * HEIGHT, :] = v.astype(out.dtype)
                return carry

            lax.fori_loop(0, LB // some, mixing, 0)

    for c in range(CHUNKS):
        for copies, hops in ring.values():
            for k in range(hops):
                for item in copies(c, k):
                    item.wait_send()
        h_copy(c).wait_send()


def vmem():
    return pl.BlockSpec(memory_space=pltpu.VMEM)


def smem():
    return pl.BlockSpec(memory_space=pltpu.SMEM)


def local(
    source_feats, rel_weight, tiles, src_blk, rel_id, owner, local_blk, in_degree, mix_weight, bias
):
    n_rows = lax.axis_size("rows")
    src_dev, half_w = source_feats.shape
    tile = tiles.shape[1]
    parts, per_row = src_blk.shape
    n_rel = rel_weight.shape[0]
    n_src_blocks = src_dev // tile
    n_local = in_degree.shape[0] // tile

    key = jnp.zeros((8, 128), jnp.int32).at[0, :parts].set(owner[:, 0] * LB + local_blk)
    picks = (rel_id * n_src_blocks + src_blk).reshape(-1)
    n_hops = NZ + NX + NY - 3
    part, keys = pl.pallas_call(
        partials_kernel,
        out_shape=(
            jax.ShapeDtypeStruct((CHUNKS, parts, HEIGHT, COLS), jnp.bfloat16),
            jax.ShapeDtypeStruct((NY, NX, NZ, 8, 128), jnp.int32),
        ),
        in_specs=[smem(), vmem(), vmem(), vmem(), vmem()],
        out_specs=(vmem(), vmem()),
        scratch_shapes=[
            pltpu.VMEM((n_rel * n_src_blocks, tile, half_w), jnp.bfloat16),
            pltpu.SemaphoreType.DMA((n_hops,)),
            pltpu.SemaphoreType.DMA((n_hops,)),
        ],
        compiler_params=pltpu.CompilerParams(collective_id=1, has_side_effects=True),
    )(picks, key, source_feats, rel_weight[:, 0], tiles)
    keys = keys[:, :, :, 0, :parts].transpose(2, 1, 0, 3).reshape(n_rows, parts)
    z_tab, x_tab, y_tab, fits = tables(keys, lax.axis_index("rows"))
    degree = in_degree.astype(jnp.float32)

    def routed(part):
        wide = jnp.broadcast_to(degree[:, None], (degree.shape[0], COLS)).reshape(n_local, tile, COLS)
        block = lambda n: [pltpu.VMEM((n, HEIGHT, COLS), jnp.bfloat16)] * CHUNKS
        dma = pltpu.SemaphoreType.DMA
        out = pl.pallas_call(
            functools.partial(route_kernel, schedule()),
            out_shape=jax.ShapeDtypeStruct((n_local, tile, half_w), jnp.bfloat16),
            in_specs=[smem(), smem(), smem()] + [vmem()] * 4,
            out_specs=vmem(),
            scratch_shapes=block(2 * Z_CAP[0])
            + block(Z_SLOTS)
            + block(2 * X_CAP[0])
            + block(X_SLOTS)
            + block(2 * Y_CAP[0])
            + block(Y_SLOTS)
            + block(2 * R_LIST)
            + block(2 * R_LIST + 2 * FAR + GROUP)
            + [pltpu.VMEM((2, n_local, HEIGHT, COLS), jnp.bfloat16)] * CHUNKS
            + [
                pltpu.VMEM((MERGE + 1, HEIGHT, COLS), jnp.bfloat16),
                pltpu.VMEM((n_local, HEIGHT, half_w), jnp.float32),
                dma((CHUNKS, len(Z_CAP), 2)),
                dma((CHUNKS, len(Z_CAP), 2)),
                dma((CHUNKS, len(X_CAP), 2)),
                dma((CHUNKS, len(X_CAP), 2)),
                dma((CHUNKS, len(Y_CAP), 2)),
                dma((CHUNKS, len(Y_CAP), 2)),
                dma((CHUNKS, 2, 2)),
                dma((CHUNKS, 2, 2)),
                dma((CHUNKS,)),
                dma((CHUNKS,)),
            ],
            compiler_params=pltpu.CompilerParams(
                collective_id=0, has_side_effects=True, vmem_limit_bytes=64 * 1024 * 1000
            ),
        )(z_tab, x_tab, y_tab, part, wide, mix_weight, bias[None, :])
        return out.reshape(n_local * tile, half_w)

    def dense(part):
        capacity = max(2, 2 * parts // n_rows)
        partials = part.reshape(ROW_CHUNKS, COL_CHUNKS, parts, HEIGHT, COLS)
        partials = partials.transpose(2, 0, 3, 1, 4).reshape(parts, tile * half_w)
        target_dev = owner[:, 0]
        positions = jnp.arange(parts, dtype=jnp.int32)
        earlier = (target_dev[:, None] == target_dev[None, :]) & (
            positions[None, :] < positions[:, None]
        )
        rank = jnp.sum(earlier.astype(jnp.int32), axis=1)
        slot = target_dev * capacity + rank
        slot_ids = jnp.arange(n_rows * capacity, dtype=jnp.int32)
        placing = slot_ids[:, None] == slot[None, :]
        outgoing = jnp.dot(
            placing.astype(jnp.bfloat16), partials, preferred_element_type=jnp.float32
        ).astype(jnp.bfloat16)
        out_ids = jnp.sum(jnp.where(placing, local_blk[None, :] + 1, 0), axis=1) - 1
        block_index = jnp.arange(n_local, dtype=jnp.int32)
        arrived = lax.all_to_all(outgoing, "rows", split_axis=0, concat_axis=0, tiled=True)
        arrived_ids = lax.all_to_all(out_ids, "rows", split_axis=0, concat_axis=0, tiled=True)
        selector = (arrived_ids[None, :] == block_index[:, None]).astype(jnp.bfloat16)
        summed = jnp.dot(selector, arrived, preferred_element_type=jnp.float32)
        summed = summed.reshape(n_local * tile, half_w)
        agg = (summed / degree[:, None]).astype(jnp.bfloat16)
        theirs = lax.ppermute(agg, "half", [(0, 1), (1, 0)])
        half = lax.axis_index("half")
        w_mine = lax.dynamic_slice_in_dim(mix_weight, half * half_w, half_w, 0)
        w_theirs = lax.dynamic_slice_in_dim(mix_weight, (1 - half) * half_w, half_w, 0)
        mixed = jnp.dot(
            jnp.concatenate([agg, theirs], axis=1),
            jnp.concatenate([w_mine, w_theirs], axis=0),
            preferred_element_type=jnp.float32,
        )
        return jax.nn.relu(mixed + bias).astype(jnp.bfloat16)

    return lax.cond(fits, routed, dense, part)


def solution(mesh):
    placed = (
        P("rows", "half"),
        P(None, "half", None, None),
        P("rows", None, None),
        P("rows", None),
        P("rows", None),
        P("rows", None),
        P("rows"),
        P("rows"),
        P(None, "half"),
        P("half"),
    )
    return jax.shard_map(
        local, mesh=mesh, in_specs=placed, out_specs=P("rows", "half"), check_vma=False
    )
```

```python
import functools

import jax
import jax.numpy as jnp
from jax import lax
from jax.experimental import pallas as pl
from jax.experimental.pallas import tpu as pltpu
from jax.sharding import PartitionSpec as P

MESH = pl.DeviceIdType.MESH
NZ, NX, NY = 8, 4, 4
ROWS = NZ * NX * NY
TILE = 64
LB = 32

Z_LOCAL, Z_CAP = 12, (24, 20, 14, 6)
X_LOCAL, X_CAP = 32, (34, 15)
MERGE = 96
Y_CAP = (26, 12)
GROUP = LB // NX
FAR = GROUP // 2
R_LIST = GROUP + FAR

COLS = 128
HEIGHT = 32
COL_CHUNKS = 4
ROW_CHUNKS = TILE // HEIGHT
CHUNKS = COL_CHUNKS * ROW_CHUNKS


def bases(local, caps, start):
    right, left, at = [], [], start + local
    for cap in caps:
        right.append(at)
        at += cap
    for cap in caps:
        left.append(at)
        at += cap
    return right, left, at


Z_RIGHT, Z_LEFT, Z_SLOTS = bases(Z_LOCAL, Z_CAP, 0)
X_RIGHT, X_LEFT, X_SLOTS = bases(X_LOCAL, X_CAP, 1)
Y_RIGHT, Y_LEFT, Y_SLOTS = bases(LB, Y_CAP, 1)


def ones_where(mask):
    return jnp.where(mask, 1.0, 0.0).astype(jnp.bfloat16)


def iota(shape, axis):
    return lax.broadcasted_iota(jnp.int32, shape, axis)


def dot32(a, b, transposed=False):
    dims = (((1,), (1 if transposed else 0,)), ((), ()))
    v = lax.dot_general(
        a.astype(jnp.bfloat16), b.astype(jnp.bfloat16), dims, preferred_element_type=jnp.float32
    )
    return v.astype(jnp.int32)


def tables(k, me):
    mz, mx, my = me // (NX * NY), (me // NY) % NX, me % NY
    n, seg = 128, LB
    wide = (n, n)
    low, col = iota(wide, 0), iota(wide, 1)
    same = (low // seg) == (col // seg)
    tri_all = ones_where(low < col)
    tri_seg = ones_where((low < col) & same)
    sum_seg = ones_where(same)
    shape = k.shape
    lane, row = iota(shape, 1), iota(shape, 0)
    owner, block = k // LB, k % LB
    dz, dy = owner // (NX * NY), owner % NY
    home, spare = block // GROUP, (owner // NY) % NX * GROUP + block % GROUP
    sz, sy, sx, p = row % NZ, row // NZ, lane // seg, lane % seg

    def number(mask):
        return jnp.where(mask, 1, 0)

    def listed(delta, ring, starts, right_base, left_base, local_base, before, total):
        half = ring // 2
        odd = before([delta == half])[0] % 2
        to_right = ((delta >= 1) & (delta < half)) | ((delta == half) & (odd == 0))
        to_left = ((delta > half) & (delta < ring)) | ((delta == half) & (odd == 1))
        dist = jnp.where(delta <= half, delta, ring - delta)
        masks = [delta == 0]
        masks += [to_right & (dist == h) for h in range(1, half + 1)]
        masks += [to_left & (dist == h) for h in range(1, half + 1)]
        ranks, totals = before(masks), total(masks)
        address = jnp.where(masks[0], local_base + ranks[0], 0)
        slot = jnp.where(masks[0], starts[0] + ranks[0], n)
        worst = []
        for side, base in ((0, right_base), (1, left_base)):
            farther = jnp.zeros_like(totals[0])
            for h in range(half, 0, -1):
                at = 1 + side * half + h - 1
                address = jnp.where(masks[at], base[h - 1] + farther + ranks[at], address)
                slot = jnp.where(masks[at], starts[1 + side] + farther + ranks[at], slot)
                farther = farther + totals[at]
                worst.append((h - 1, farther))
        return address, slot, totals[0], worst

    def stacked(masks, matrix):
        v = dot32(jnp.concatenate([ones_where(m) for m in masks], axis=0), matrix)
        rows = masks[0].shape[0]
        return [v[i * rows : (i + 1) * rows] for i in range(len(masks))]

    def overflow(kept, local, worst, caps):
        bad = number(kept > local)
        for h, count in worst:
            bad = bad | number(count > caps[h])
        return bad

    z_addr, z_slot, z_kept, z_worst = listed(
        (dz + NZ - sz) % NZ, NZ, (0, Z_LOCAL, Z_LOCAL + Z_CAP[0]), Z_RIGHT, Z_LEFT, 0,
        lambda m: stacked(m, tri_seg), lambda m: stacked(m, sum_seg),
    )
    bad = overflow(z_kept, Z_LOCAL, z_worst, Z_CAP)

    def placed(values, slots, valid):
        hit = ones_where(jnp.broadcast_to(jnp.where(valid, slots, n), wide) == low)
        return dot32(values, hit, True)

    def pick(a, index, count):
        total = jnp.zeros_like(a[:1])
        for i in range(count):
            total = jnp.where(index == i, a[i : i + 1], total)
        return total

    def pick_y(a):
        total = jnp.zeros_like(a[:NZ])
        for i in range(NY):
            total = jnp.where(my == i, a[i * NZ : (i + 1) * NZ], total)
        return total

    lane8 = iota((NZ, n), 1)
    own = pick(pick_y(z_slot), mz, NZ)
    z_tab = placed(lane8[:1] % seg, own, lane8[:1] // seg == mx)

    def before_x(masks):
        inner, whole = stacked(masks, tri_seg), stacked(masks, sum_seg)
        r, c = iota((NZ, NZ), 0), iota((NZ, NZ), 1)
        lower = ones_where(c < r)
        groups = masks[0].shape[0] // NZ
        outer = [
            jnp.concatenate([dot32(lower, w[g * NZ : (g + 1) * NZ]) for g in range(groups)], axis=0)
            for w in whole
        ]
        return [a + b for a, b in zip(inner, outer)]

    def total_x(masks):
        whole = stacked(masks, sum_seg)
        groups = masks[0].shape[0] // NZ
        return [
            jnp.concatenate(
                [
                    jnp.broadcast_to(
                        jnp.sum(w[g * NZ : (g + 1) * NZ], axis=0, keepdims=True), (NZ, n)
                    )
                    for g in range(groups)
                ],
                axis=0,
            )
            for w in whole
        ]

    dz8, home8, dy8, spare8 = pick_y(dz), pick_y(home), pick_y(dy), pick_y(spare)
    here = dz8 == mz
    x_addr, x_slot, _, _ = listed(
        jnp.where(here, (home8 + NX - lane8 // seg) % NX, NX), NX,
        (0, X_LOCAL, X_LOCAL + X_CAP[0]), X_RIGHT, X_LEFT, 1, before_x, total_x,
    )
    z_addr8 = pick_y(z_addr)
    x_tab = jnp.zeros((1, n), jnp.int32)
    for z in range(NZ):
        x_tab = x_tab + placed(
            z_addr8[z : z + 1], x_slot[z : z + 1], here[z : z + 1] & (lane8[:1] // seg == mx)
        )
    for z in range(NZ):
        deltas = [(dz == z) & ((home + NX - sx) % NX == d) for d in range(NX)]
        kept, right, tied, left = total_x(deltas)
        near, far = tied // 2, (tied + 1) // 2
        bad = bad | overflow(kept, X_LOCAL, [(1, far), (0, far + right), (0, near + left)], X_CAP)

    spots = dz * NX + home
    wanted = (dy + NY - sy) % NY * LB + spare
    hists = []
    holder = iota((NZ * NX, n), 0)
    for y in range(NY):
        total = jnp.zeros((NZ * NX, n), jnp.int32)
        for z in range(NZ):
            r = y * NZ + z
            holds = ones_where(jnp.broadcast_to(spots[r : r + 1], (NZ * NX, n)) == holder)
            wants = ones_where(jnp.broadcast_to(wanted[r : r + 1], wide) == low)
            total = total + dot32(holds, wants, True)
        hists.append(total)
        count = jnp.sum(total, axis=1, keepdims=True)
        bad = bad | number(jnp.broadcast_to(count, total.shape) > MERGE)
        present = dot32(ones_where(total > 0), sum_seg)
        group = iota(total.shape, 1) // seg
        tied = present
        bad = bad | number((group == 1) & (present > Y_CAP[0]))
        bad = bad | number((group == 3) & (present > Y_CAP[0]))
        bad = bad | number((group == 2) & ((present + 1) // 2 > Y_CAP[1]))
        ties = ones_where((total > 0) & (group == 2))
        every = dot32(ties, jnp.ones(wide, jnp.bfloat16))
        bad = bad | number((group == 1) & (present + (every + 1) // 2 > Y_CAP[0]))
        bad = bad | number((group == 3) & (present + every // 2 > Y_CAP[0]))
    index = mz * NX + mx
    lines = []
    for y in range(NY):
        mine = iota((NZ * NX, n), 0) == index
        lines.append(jnp.sum(jnp.where(mine, hists[y], 0), axis=0, keepdims=True))
    pad = [jnp.zeros((1, n), jnp.int32)] * (NZ - NY)
    line = jnp.concatenate(lines + pad, axis=0)
    ones_all = jnp.ones(wide, jnp.bfloat16)
    y_addr, y_slot, _, _ = listed(
        jnp.where(line > 0, lane8 // seg, NY), NY, (n, 0, Y_CAP[0]), Y_RIGHT, Y_LEFT, 1,
        lambda m: stacked(m, tri_all), lambda m: stacked(m, ones_all),
    )
    hist = pick(line, my, NY)
    start = dot32(hist, tri_all)
    last = jnp.where(hist > 0, start + hist - 1, MERGE)
    y_lists = placed(last, pick(y_slot, my, NY), hist > 0)
    finals = jnp.zeros((1, n), jnp.int32)
    for hop in range(1, NY):
        source = (my + NY - hop) % NY
        there = jnp.where(pick(line, source, NY) > 0, pick(y_addr, source, NY), 0)
        finals = jnp.where(lane8[:1] // seg == hop, there, finals)

    arrived = here & (home8 == mx)
    wanted8 = (dy8 + NY - my) % NY * LB + spare8
    y_src = jnp.zeros((1, n), jnp.int32)
    y_first = jnp.zeros((1, n), jnp.int32)
    ahead = start
    for z in range(NZ):
        valid = arrived[z : z + 1]
        hot = ones_where(jnp.broadcast_to(jnp.where(valid, wanted8[z : z + 1], n), wide) == low)
        inner = dot32(hot, tri_all)
        rank = jnp.sum(jnp.where(hot > 0, inner, 0), axis=0, keepdims=True)
        seat = dot32(ahead, hot) + rank
        first = ones_where(seat == dot32(start, hot))
        y_src = y_src + placed(x_addr[z : z + 1], seat, valid)
        y_first = y_first + placed(first, seat, valid)
        ahead = ahead + dot32(jnp.ones((1, n), jnp.bfloat16), hot, True)
    flag = jnp.max(bad.astype(jnp.float32), axis=(0, 1), keepdims=True).astype(jnp.int32)
    flag = jnp.broadcast_to(flag, (1, n))
    z_tab = jnp.minimum(z_tab, seg - 1)
    x_tab = jnp.minimum(x_tab, Z_SLOTS - 1)
    y_src = jnp.minimum(y_src, X_SLOTS - 1)
    last = jnp.minimum(last, MERGE)
    y_lists = jnp.minimum(y_lists, MERGE)
    finals = jnp.minimum(finals, Y_SLOTS - 1)
    return jnp.concatenate([z_tab, x_tab, y_src, y_first, last, y_lists, finals, flag], axis=0)


def messages(r, feats, weight, msgs):
    step, per = 256, feats.shape[0] // TILE
    for s in range(feats.shape[0] // step):
        m = jnp.dot(
            feats[s * step : (s + 1) * step, :], weight[r], preferred_element_type=jnp.float32
        ).astype(jnp.bfloat16)
        spot = r * per + s * (step // TILE)
        msgs[spot : spot + step // TILE] = m.reshape(step // TILE, TILE, m.shape[1])


def partial_of(p, picks, tiles, msgs):
    kt = tiles.shape[2] // TILE
    rhs = jnp.concatenate([msgs[picks[p * kt + k]] for k in range(kt)], axis=0)
    return jnp.dot(tiles[p], rhs, preferred_element_type=jnp.float32).astype(jnp.bfloat16)


def partials_kernel(picks, feats, weight, tiles, out, msgs):
    for r in range(weight.shape[0]):
        messages(r, feats, weight, msgs)

    def one(p, carry):
        out[p] = partial_of(p, picks, tiles, msgs)
        return carry

    lax.fori_loop(0, tiles.shape[0], one, 0)


def schedule():
    unit = 1.58 / CHUNKS
    links = {"z": "z", "x": "x", "y": "y", "r": "x"}
    sends = {
        "z": [c * unit for c in Z_CAP],
        "x": [c * unit for c in X_CAP],
        "y": [c * unit for c in Y_CAP],
        "r": [R_LIST * unit, FAR * unit],
    }
    stages = ["z", "x", "y", "r", "g"]
    work = {"z": 0.5, "x": 0.5, "y": 1.2, "r": 0.7, "g": 1.2}
    free = {"z": 0.0, "x": 0.0, "y": 0.0, "h": 0.0}
    now, order = 0.0, []
    ready = {("z", 0, c): 0.0 for c in range(CHUNKS)}
    begun = 0
    while ready:
        best = None
        for (kind, k, c), t in ready.items():
            start = max(t, now)
            if kind == "z" and k == 0:
                start = max(start, free["z"] - 2.5)
            rank = (start, 0 if k > 0 else 1, c, -stages.index(kind))
            if best is None or rank < best[0]:
                best = (rank, (kind, k, c), start)
        _, (kind, k, c), start = best
        del ready[(kind, k, c)]
        order.append((kind, k, c))
        begun += (kind, k) == ("z", 0)
        if begun == 2:
            order.append(("t", 0, 0))
            start, begun = start + 5.0, 3
        now = start + (work[kind] if k == 0 else 0.1)
        if kind == "g":
            continue
        if k < len(sends[kind]):
            link = links[kind]
            free[link] = max(free[link], now) + sends[kind][k]
            ready[(kind, k + 1, c)] = free[link] + 1.8
        elif kind == "r":
            now += 0.7
            free["h"] = max(free["h"], now) + 0.8
            ready[("g", 0, c)] = free["h"] + 1.0
        else:
            ready[(stages[stages.index(kind) + 1], 0, c)] = now
    return order


def rings(me):
    mz, mx, my = me // (NX * NY), (me // NY) % NX, me % NY

    def at(z, x, y):
        return {"rows": (z % NZ) * (NX * NY) + (x % NX) * NY + y % NY}

    along_z = [at(mz + k, mx, my) for k in range(1, NZ)]
    along_x = [at(mz, mx + k, my) for k in range(1, NX)]
    along_y = [at(mz, mx, my + k) for k in range(1, NY)]
    return mz, mx, my, along_z, along_x, along_y


def copy(src, dst, send, recv, device):
    return pltpu.make_async_remote_copy(
        src_ref=src, dst_ref=dst, send_sem=send, recv_sem=recv,
        device_id=device, device_id_type=MESH,
    )


def front_kernel(picks, key, feats, weight, tiles, part, tab, msgs, keys, k_send, k_recv):
    me = lax.axis_index("rows")
    mz, mx, my, to_z, to_x, to_y = rings(me)
    hops = to_z + to_x + to_y
    barrier = pltpu.get_barrier_semaphore()
    for device in hops:
        pl.semaphore_signal(barrier, inc=1, device_id=device, device_id_type=MESH)

    def key_copies(first, n, src, dst):
        return [
            copy(src, dst, k_send.at[i], k_recv.at[i], hops[i]) for i in range(first, first + n)
        ]

    along_z = key_copies(0, NZ - 1, key, keys.at[my, mx, mz])
    along_x = key_copies(NZ - 1, NX - 1, keys.at[my, mx], keys.at[my, mx])
    along_y = key_copies(NZ + NX - 2, NY - 1, keys.at[my], keys.at[my])

    def begin(items):
        for item in items:
            item.start()

    def landed(items):
        for item in items:
            item.wait_recv()

    keys[my, mx, mz] = key[...]
    messages(0, feats, weight, msgs)
    pl.semaphore_wait(barrier, len(hops))
    begin(along_z)
    for r in range(1, weight.shape[0]):
        messages(r, feats, weight, msgs)

    def one(p, carry):
        v = partial_of(p, picks, tiles, msgs)
        for i in range(ROW_CHUNKS):
            for j in range(COL_CHUNKS):
                part[i * COL_CHUNKS + j, p] = v[
                    i * HEIGHT : (i + 1) * HEIGHT, j * COLS : (j + 1) * COLS
                ]
        return carry

    parts = tiles.shape[0]
    lax.fori_loop(0, parts // 4, one, 0)
    landed(along_z)
    begin(along_x)
    lax.fori_loop(parts // 4, 5 * parts // 8, one, 0)
    landed(along_x)
    begin(along_y)
    lax.fori_loop(5 * parts // 8, parts, one, 0)
    landed(along_y)

    def add_up(y):
        def body(i, held):
            return held + keys[y, i // NZ, i % NZ]

        return lax.fori_loop(0, NX * NZ, body, jnp.zeros((8, 128), jnp.int32), unroll=4)

    tab[...] = tables(jnp.concatenate([add_up(y) for y in range(NY)], axis=0), me)
    for item in along_z + along_x + along_y:
        item.wait_send()


def route_kernel(order, *refs):
    it = iter(refs)
    tab, part, counts, mix, bias, out = [next(it) for _ in range(6)]
    zs = [next(it) for _ in range(CHUNKS)]
    zb = [next(it) for _ in range(CHUNKS)]
    xs = [next(it) for _ in range(CHUNKS)]
    xb = [next(it) for _ in range(CHUNKS)]
    ys = [next(it) for _ in range(CHUNKS)]
    yb = [next(it) for _ in range(CHUNKS)]
    rs = [next(it) for _ in range(CHUNKS)]
    rb = [next(it) for _ in range(CHUNKS)]
    ag = [next(it) for _ in range(CHUNKS)]
    stage, total, degree = next(it), next(it), next(it)
    z_sems, x_sems, y_sems, r_sems = [(next(it), next(it)) for _ in range(4)]
    h_send, h_recv = next(it), next(it)

    me, half = lax.axis_index("rows"), lax.axis_index("half")
    mz, mx, my, to_z, to_x, to_y = rings(me)
    zp, zm, xp, xm, yp, ym = to_z[0], to_z[-1], to_x[0], to_x[-1], to_y[0], to_y[-1]
    other = {"half": 1 - half}
    barrier = pltpu.get_barrier_semaphore()
    neighbours = (zp, zm, xp, xm, yp, ym, other)
    for device in neighbours:
        pl.semaphore_signal(barrier, inc=1, device_id=device, device_id_type=MESH)
    pl.semaphore_wait(barrier, len(neighbours))

    def gather(dst, base, read, entry, n):
        def body(j, carry):
            dst[base + j] = read(entry(j))
            return carry

        lax.fori_loop(0, n, body, 0, unroll=4)

    def hop_copies(sent, held, sems, forward, backward, caps, right, left):
        def copies(c, k):
            n = caps[k]
            result = []
            for side, device, base in ((0, forward, right), (1, backward, left)):
                if k == 0:
                    src = sent[c].at[pl.ds(side * n, n)]
                else:
                    src = held[c].at[pl.ds(base[k - 1], n)]
                dst = held[c].at[pl.ds(base[k], n)]
                result.append(copy(src, dst, sems[0].at[c, k, side], sems[1].at[c, k, side], device))
            return result

        return copies, len(caps)

    def h_copy(c):
        return copy(ag[c].at[half], ag[c].at[half], h_send.at[c], h_recv.at[c], other)

    stage[MERGE] = jnp.zeros(stage.shape[1:], stage.dtype)
    for c in range(CHUNKS):
        xb[c][0] = jnp.zeros(xb[c].shape[1:], xb[c].dtype)
        yb[c][0] = jnp.zeros(yb[c].shape[1:], yb[c].dtype)

    ring = {
        "z": hop_copies(zs, zb, z_sems, zp, zm, Z_CAP, Z_RIGHT, Z_LEFT),
        "x": hop_copies(xs, xb, x_sems, xp, xm, X_CAP, X_RIGHT, X_LEFT),
        "y": hop_copies(ys, yb, y_sems, yp, ym, Y_CAP, Y_RIGHT, Y_LEFT),
        "r": hop_copies(rs, rb, r_sems, xp, xm, (R_LIST, FAR), (0, 2 * R_LIST), (R_LIST, 2 * R_LIST + FAR)),
    }
    Z_TAB, X_TAB, Y_SRC, Y_FIRST, LAST, LISTS, FINALS = range(7)

    for kind, k, c in order:
        row, col = c // COL_CHUNKS, c % COL_CHUNKS
        if kind == "t":
            eye = iota((128, 128), 0) == iota((128, 128), 1)
            per = 128 // TILE
            for i in range(LB // per):
                one_row = jnp.broadcast_to(counts[i : i + 1].astype(jnp.float32), (128, 128))
                spread = jnp.dot(
                    jnp.where(eye, one_row, 0.0).astype(jnp.bfloat16),
                    jnp.ones((128, COLS), jnp.bfloat16),
                    preferred_element_type=jnp.float32,
                )
                degree[i * per : (i + 1) * per] = spread.reshape(per, TILE, COLS)
        elif kind in ring and k > 0:
            copies, hops = ring[kind]
            for item in copies(c, k - 1):
                item.wait_recv()
            if k < hops:
                for item in copies(c, k):
                    item.start()
            elif kind == "r":

                def finish(base, first, n):
                    def body(i, carry):
                        b = first + i
                        v = rb[c][base + i].astype(jnp.float32)
                        v = v / degree[b, row * HEIGHT : (row + 1) * HEIGHT, :]
                        ag[c][half, b] = v.astype(jnp.bfloat16)
                        return carry

                    lax.fori_loop(0, n, body, 0, unroll=4)

                far = 2 * R_LIST
                finish(far + 2 * FAR, mx * GROUP, GROUP)
                finish(FAR, (mx + NX - 1) % NX * GROUP, GROUP)
                finish(R_LIST + FAR, (mx + 1) % NX * GROUP, GROUP)
                finish(far, (mx + 2) % NX * GROUP, GROUP)
                h_copy(c).start()
        elif kind == "z":
            read = lambda i: part[c, i]
            gather(zs[c], 0, read, lambda j: tab[Z_TAB, Z_LOCAL + j], 2 * Z_CAP[0])
            for item in ring["z"][0](c, 0):
                item.start()
            gather(zb[c], 0, read, lambda j: tab[Z_TAB, j], Z_LOCAL)
        elif kind == "x":
            read = lambda i: zb[c][i]
            gather(xs[c], 0, read, lambda j: tab[X_TAB, X_LOCAL + j], 2 * X_CAP[0])
            for item in ring["x"][0](c, 0):
                item.start()
            gather(xb[c], 1, read, lambda j: tab[X_TAB, j], X_LOCAL)
        elif kind == "y":

            def add(j, total_now):
                v = xb[c][tab[Y_SRC, j]].astype(jnp.float32)
                total_now = jnp.where(tab[Y_FIRST, j] > 0, v, total_now + v)
                stage[j] = total_now.astype(stage.dtype)
                return total_now

            lax.fori_loop(0, MERGE, add, jnp.zeros((HEIGHT, COLS), jnp.float32), unroll=4)
            read = lambda i: stage[i]
            gather(ys[c], 0, read, lambda j: tab[LISTS, j], 2 * Y_CAP[0])
            for item in ring["y"][0](c, 0):
                item.start()
            gather(yb[c], 1, read, lambda j: tab[LAST, j], LB)
        elif kind == "r":

            def collect(dst, base, hop, first, n):
                group = (mx + hop) % NX * GROUP + first

                def body(i, carry):
                    q = group + i
                    v = yb[c][1 + q].astype(jnp.float32)
                    for other_y in range(NY - 1):
                        v = v + yb[c][tab[FINALS, (other_y + 1) * LB + q]].astype(jnp.float32)
                    dst[base + i] = v.astype(dst.dtype)
                    return carry

                lax.fori_loop(0, n, body, 0, unroll=4)

            collect(rs[c], 0, 2, 0, FAR)
            collect(rs[c], FAR, 1, 0, GROUP)
            collect(rs[c], R_LIST, 2, FAR, FAR)
            collect(rs[c], R_LIST + FAR, NX - 1, 0, GROUP)
            for item in ring["r"][0](c, 0):
                item.start()
            collect(rb[c], 2 * R_LIST + 2 * FAR, 0, 0, GROUP)
        else:
            h_copy(c).wait_recv()
            some = 8
            width = mix.shape[0] // 2
            w = jnp.concatenate(
                [
                    mix[col * COLS : (col + 1) * COLS, :],
                    mix[width + col * COLS : width + (col + 1) * COLS, :],
                ],
                axis=0,
            )

            def mixing(b, carry):
                blocks = pl.ds(b * some, some)
                a = jnp.concatenate(
                    [
                        ag[c][0, blocks].reshape(some * HEIGHT, COLS),
                        ag[c][1, blocks].reshape(some * HEIGHT, COLS),
                    ],
                    axis=1,
                )
                v = jnp.dot(a, w, preferred_element_type=jnp.float32)
                v = v.reshape(some, HEIGHT, v.shape[1])
                if col > 0:
                    v = v + total[blocks]
                if col < COL_CHUNKS - 1:
                    total[blocks] = v
                else:
                    v = jnp.maximum(v + bias[...][None], 0.0)
                    out[blocks, row * HEIGHT : (row + 1) * HEIGHT, :] = v.astype(out.dtype)
                return carry

            lax.fori_loop(0, LB // some, mixing, 0)

    for c in range(CHUNKS):
        for copies, hops in ring.values():
            for k in range(hops):
                for item in copies(c, k):
                    item.wait_send()
        h_copy(c).wait_send()


def vmem():
    return pl.BlockSpec(memory_space=pltpu.VMEM)


def smem():
    return pl.BlockSpec(memory_space=pltpu.SMEM)


def local(
    source_feats, rel_weight, tiles, src_blk, rel_id, owner, local_blk, in_degree, mix_weight, bias
):
    n_rows = lax.axis_size("rows")
    src_dev, half_w = source_feats.shape
    tile = tiles.shape[1]
    parts, per_row = src_blk.shape
    n_rel = rel_weight.shape[0]
    n_src_blocks = src_dev // tile
    n_local = in_degree.shape[0] // tile

    me = lax.axis_index("rows")
    spot_z = lax.broadcasted_iota(jnp.int32, (NZ, 128), 0) == me // (NX * NY)
    spot_x = lax.broadcasted_iota(jnp.int32, (NZ, 128), 1) // LB == (me // NY) % NX
    own = jnp.tile(owner[:, 0] * LB + local_blk, 128 // parts)
    key = jnp.where(spot_z & spot_x, own[None, :], 0)
    weight = rel_weight.reshape(n_rel, half_w, half_w)
    picks = (rel_id * n_src_blocks + src_blk).reshape(-1)
    n_hops = NZ + NX + NY - 3
    degree = in_degree.astype(jnp.float32)
    block = lambda n: [pltpu.VMEM((n, HEIGHT, COLS), jnp.bfloat16)] * CHUNKS
    dma = pltpu.SemaphoreType.DMA
    pair = lambda n: [dma((CHUNKS, n, 2)), dma((CHUNKS, n, 2))]
    part, tab = pl.pallas_call(
        front_kernel,
        out_shape=(
            jax.ShapeDtypeStruct((CHUNKS, parts, HEIGHT, COLS), jnp.bfloat16),
            jax.ShapeDtypeStruct((8, 128), jnp.int32),
        ),
        in_specs=[smem()] + [vmem()] * 4,
        out_specs=(vmem(), vmem()),
        scratch_shapes=[
            pltpu.VMEM((n_rel * n_src_blocks, tile, half_w), jnp.bfloat16),
            pltpu.VMEM((NY, NX, NZ, 8, 128), jnp.int32),
            dma((n_hops,)),
            dma((n_hops,)),
        ],
        compiler_params=pltpu.CompilerParams(collective_id=1, has_side_effects=True),
    )(picks, key, source_feats, weight, tiles)

    def routed():
        out = pl.pallas_call(
            functools.partial(route_kernel, schedule()),
            out_shape=jax.ShapeDtypeStruct((n_local, tile, half_w), jnp.bfloat16),
            in_specs=[smem()] + [vmem()] * 4,
            out_specs=vmem(),
            scratch_shapes=block(2 * Z_CAP[0])
            + block(Z_SLOTS)
            + block(2 * X_CAP[0])
            + block(X_SLOTS)
            + block(2 * Y_CAP[0])
            + block(Y_SLOTS)
            + block(2 * R_LIST)
            + block(2 * R_LIST + 2 * FAR + GROUP)
            + [pltpu.VMEM((2, n_local, HEIGHT, COLS), jnp.bfloat16)] * CHUNKS
            + [
                pltpu.VMEM((MERGE + 1, HEIGHT, COLS), jnp.bfloat16),
                pltpu.VMEM((n_local, HEIGHT, half_w), jnp.float32),
                pltpu.VMEM((n_local, tile, COLS), jnp.float32),
            ]
            + pair(len(Z_CAP))
            + pair(len(X_CAP))
            + pair(len(Y_CAP))
            + pair(2)
            + [dma((CHUNKS,)), dma((CHUNKS,))],
            compiler_params=pltpu.CompilerParams(
                collective_id=0, has_side_effects=True, vmem_limit_bytes=67043328
            ),
        )(tab, part, in_degree.reshape(-1, 128), mix_weight, bias[None, :])
        return out.reshape(n_local * tile, half_w)

    def dense():
        partials = pl.pallas_call(
            partials_kernel,
            out_shape=jax.ShapeDtypeStruct((parts, tile, half_w), jnp.bfloat16),
            in_specs=[smem(), vmem(), vmem(), vmem()],
            out_specs=vmem(),
            scratch_shapes=[pltpu.VMEM((n_rel * n_src_blocks, tile, half_w), jnp.bfloat16)],
        )(picks, source_feats, weight, tiles).reshape(parts, tile * half_w)
        capacity = max(2, 2 * parts // n_rows)
        target_dev = owner[:, 0]
        positions = jnp.arange(parts, dtype=jnp.int32)
        earlier = (target_dev[:, None] == target_dev[None, :]) & (
            positions[None, :] < positions[:, None]
        )
        rank = jnp.sum(earlier.astype(jnp.int32), axis=1)
        slot = target_dev * capacity + rank
        slot_ids = jnp.arange(n_rows * capacity, dtype=jnp.int32)
        placing = slot_ids[:, None] == slot[None, :]
        outgoing = jnp.dot(
            placing.astype(jnp.bfloat16), partials, preferred_element_type=jnp.float32
        ).astype(jnp.bfloat16)
        out_ids = jnp.sum(jnp.where(placing, local_blk[None, :] + 1, 0), axis=1) - 1
        block_index = jnp.arange(n_local, dtype=jnp.int32)
        arrived = lax.all_to_all(outgoing, "rows", split_axis=0, concat_axis=0, tiled=True)
        arrived_ids = lax.all_to_all(out_ids, "rows", split_axis=0, concat_axis=0, tiled=True)
        selector = (arrived_ids[None, :] == block_index[:, None]).astype(jnp.bfloat16)
        summed = jnp.dot(selector, arrived, preferred_element_type=jnp.float32)
        summed = summed.reshape(n_local * tile, half_w)
        agg = (summed / degree[:, None]).astype(jnp.bfloat16)
        theirs = lax.ppermute(agg, "half", [(0, 1), (1, 0)])
        half = lax.axis_index("half")
        w_mine = lax.dynamic_slice_in_dim(mix_weight, half * half_w, half_w, 0)
        w_theirs = lax.dynamic_slice_in_dim(mix_weight, (1 - half) * half_w, half_w, 0)
        mixed = jnp.dot(
            jnp.concatenate([agg, theirs], axis=1),
            jnp.concatenate([w_mine, w_theirs], axis=0),
            preferred_element_type=jnp.float32,
        )
        return jax.nn.relu(mixed + bias).astype(jnp.bfloat16)

    return lax.cond(tab[7, 0] > 0, dense, routed)


def solution(mesh):
    placed = (
        P("rows", "half"),
        P(None, "half", None, None),
        P("rows", None, None),
        P("rows", None),
        P("rows", None),
        P("rows", None),
        P("rows"),
        P("rows"),
        P(None, "half"),
        P("half"),
    )
    return jax.shard_map(
        local, mesh=mesh, in_specs=placed, out_specs=P("rows", "half"), check_vma=False
    )
```

```python
import functools

import jax
import jax.numpy as jnp
from jax import lax
from jax.experimental import pallas as pl
from jax.experimental.pallas import tpu as pltpu
from jax.sharding import PartitionSpec as P

MESH = pl.DeviceIdType.MESH
NZ, NX, NY = 8, 4, 4
ROWS = NZ * NX * NY
TILE = 64
LB = 32

Z_LOCAL, Z_CAP = 12, (24, 20, 14, 6)
X_LOCAL, X_CAP = 32, (34, 15)
MERGE = 96
Y_CAP = (26, 12)
GROUP = LB // NX
FAR = GROUP // 2
R_LIST = GROUP + FAR

COLS = 128
HEIGHT = 32
COL_CHUNKS = 4
ROW_CHUNKS = TILE // HEIGHT
CHUNKS = COL_CHUNKS * ROW_CHUNKS


def bases(local, caps, start):
    right, left, at = [], [], start + local
    for cap in caps:
        right.append(at)
        at += cap
    for cap in caps:
        left.append(at)
        at += cap
    return right, left, at


Z_RIGHT, Z_LEFT, Z_SLOTS = bases(Z_LOCAL, Z_CAP, 0)
X_RIGHT, X_LEFT, X_SLOTS = bases(X_LOCAL, X_CAP, 1)
Y_RIGHT, Y_LEFT, Y_SLOTS = bases(LB, Y_CAP, 1)


def ones_where(mask):
    return jnp.where(mask, 1.0, 0.0).astype(jnp.bfloat16)


def iota(shape, axis):
    return lax.broadcasted_iota(jnp.int32, shape, axis)


def dot32(a, b, transposed=False):
    dims = (((1,), (1 if transposed else 0,)), ((), ()))
    v = lax.dot_general(
        a.astype(jnp.bfloat16), b.astype(jnp.bfloat16), dims, preferred_element_type=jnp.float32
    )
    return v.astype(jnp.int32)


def tables(k, me, first_only=False):
    mz, mx, my = me // (NX * NY), (me // NY) % NX, me % NY
    n, seg = 128, LB
    wide = (n, n)
    low, col = iota(wide, 0), iota(wide, 1)
    same = (low // seg) == (col // seg)
    tri_all = ones_where(low < col)
    tri_seg = ones_where((low < col) & same)
    sum_seg = ones_where(same)
    shape = k.shape
    lane, row = iota(shape, 1), iota(shape, 0)
    owner, block = k // LB, k % LB
    dz, dy = owner // (NX * NY), owner % NY
    home, spare = block // GROUP, (owner // NY) % NX * GROUP + block % GROUP
    sz, sy, sx, p = row % NZ, row // NZ, lane // seg, lane % seg

    def number(mask):
        return jnp.where(mask, 1, 0)

    def listed(delta, ring, starts, right_base, left_base, local_base, before, total):
        half = ring // 2
        odd = before([delta == half])[0] % 2
        to_right = ((delta >= 1) & (delta < half)) | ((delta == half) & (odd == 0))
        to_left = ((delta > half) & (delta < ring)) | ((delta == half) & (odd == 1))
        dist = jnp.where(delta <= half, delta, ring - delta)
        masks = [delta == 0]
        masks += [to_right & (dist == h) for h in range(1, half + 1)]
        masks += [to_left & (dist == h) for h in range(1, half + 1)]
        ranks, totals = before(masks), total(masks)
        address = jnp.where(masks[0], local_base + ranks[0], 0)
        slot = jnp.where(masks[0], starts[0] + ranks[0], n)
        worst = []
        for side, base in ((0, right_base), (1, left_base)):
            farther = jnp.zeros_like(totals[0])
            for h in range(half, 0, -1):
                at = 1 + side * half + h - 1
                address = jnp.where(masks[at], base[h - 1] + farther + ranks[at], address)
                slot = jnp.where(masks[at], starts[1 + side] + farther + ranks[at], slot)
                farther = farther + totals[at]
                worst.append((h - 1, farther))
        return address, slot, totals[0], worst

    def stacked(masks, matrix):
        v = dot32(jnp.concatenate([ones_where(m) for m in masks], axis=0), matrix)
        rows = masks[0].shape[0]
        return [v[i * rows : (i + 1) * rows] for i in range(len(masks))]

    def overflow(kept, local, worst, caps):
        bad = number(kept > local)
        for h, count in worst:
            bad = bad | number(count > caps[h])
        return bad

    z_addr, z_slot, z_kept, z_worst = listed(
        (dz + NZ - sz) % NZ, NZ, (0, Z_LOCAL, Z_LOCAL + Z_CAP[0]), Z_RIGHT, Z_LEFT, 0,
        lambda m: stacked(m, tri_seg), lambda m: stacked(m, sum_seg),
    )
    bad = overflow(z_kept, Z_LOCAL, z_worst, Z_CAP)

    def placed(values, slots, valid):
        hit = ones_where(jnp.broadcast_to(jnp.where(valid, slots, n), wide) == low)
        return dot32(values, hit, True)

    def pick(a, index, count):
        total = jnp.zeros_like(a[:1])
        for i in range(count):
            total = jnp.where(index == i, a[i : i + 1], total)
        return total

    def pick_y(a):
        total = jnp.zeros_like(a[:NZ])
        for i in range(NY):
            total = jnp.where(my == i, a[i * NZ : (i + 1) * NZ], total)
        return total

    lane8 = iota((NZ, n), 1)
    own = pick(z_slot if first_only else pick_y(z_slot), mz, NZ)
    if first_only:
        z_tab = placed(lane8[:1] % seg, own, lane8[:1] // seg == mx)
        return jnp.broadcast_to(jnp.minimum(z_tab, seg - 1), (NZ, n))

    def before_x(masks):
        inner, whole = stacked(masks, tri_seg), stacked(masks, sum_seg)
        r, c = iota((NZ, NZ), 0), iota((NZ, NZ), 1)
        lower = ones_where(c < r)
        groups = masks[0].shape[0] // NZ
        outer = [
            jnp.concatenate([dot32(lower, w[g * NZ : (g + 1) * NZ]) for g in range(groups)], axis=0)
            for w in whole
        ]
        return [a + b for a, b in zip(inner, outer)]

    def total_x(masks):
        whole = stacked(masks, sum_seg)
        groups = masks[0].shape[0] // NZ
        return [
            jnp.concatenate(
                [
                    jnp.broadcast_to(
                        jnp.sum(w[g * NZ : (g + 1) * NZ], axis=0, keepdims=True), (NZ, n)
                    )
                    for g in range(groups)
                ],
                axis=0,
            )
            for w in whole
        ]

    dz8, home8, dy8, spare8 = pick_y(dz), pick_y(home), pick_y(dy), pick_y(spare)
    here = dz8 == mz
    x_addr, x_slot, _, _ = listed(
        jnp.where(here, (home8 + NX - lane8 // seg) % NX, NX), NX,
        (0, X_LOCAL, X_LOCAL + X_CAP[0]), X_RIGHT, X_LEFT, 1, before_x, total_x,
    )
    z_addr8 = pick_y(z_addr)
    x_tab = jnp.zeros((1, n), jnp.int32)
    for z in range(NZ):
        x_tab = x_tab + placed(
            z_addr8[z : z + 1], x_slot[z : z + 1], here[z : z + 1] & (lane8[:1] // seg == mx)
        )
    for z in range(NZ):
        deltas = [(dz == z) & ((home + NX - sx) % NX == d) for d in range(NX)]
        kept, right, tied, left = total_x(deltas)
        near, far = tied // 2, (tied + 1) // 2
        bad = bad | overflow(kept, X_LOCAL, [(1, far), (0, far + right), (0, near + left)], X_CAP)

    spots = dz * NX + home
    wanted = (dy + NY - sy) % NY * LB + spare
    hists = []
    holder = iota((NZ * NX, n), 0)
    for y in range(NY):
        total = jnp.zeros((NZ * NX, n), jnp.int32)
        for z in range(NZ):
            r = y * NZ + z
            holds = ones_where(jnp.broadcast_to(spots[r : r + 1], (NZ * NX, n)) == holder)
            wants = ones_where(jnp.broadcast_to(wanted[r : r + 1], wide) == low)
            total = total + dot32(holds, wants, True)
        hists.append(total)
        count = jnp.sum(total, axis=1, keepdims=True)
        bad = bad | number(jnp.broadcast_to(count, total.shape) > MERGE)
        present = dot32(ones_where(total > 0), sum_seg)
        group = iota(total.shape, 1) // seg
        tied = present
        bad = bad | number((group == 1) & (present > Y_CAP[0]))
        bad = bad | number((group == 3) & (present > Y_CAP[0]))
        bad = bad | number((group == 2) & ((present + 1) // 2 > Y_CAP[1]))
        ties = ones_where((total > 0) & (group == 2))
        every = dot32(ties, jnp.ones(wide, jnp.bfloat16))
        bad = bad | number((group == 1) & (present + (every + 1) // 2 > Y_CAP[0]))
        bad = bad | number((group == 3) & (present + every // 2 > Y_CAP[0]))
    index = mz * NX + mx
    lines = []
    for y in range(NY):
        mine = iota((NZ * NX, n), 0) == index
        lines.append(jnp.sum(jnp.where(mine, hists[y], 0), axis=0, keepdims=True))
    pad = [jnp.zeros((1, n), jnp.int32)] * (NZ - NY)
    line = jnp.concatenate(lines + pad, axis=0)
    ones_all = jnp.ones(wide, jnp.bfloat16)
    y_addr, y_slot, _, _ = listed(
        jnp.where(line > 0, lane8 // seg, NY), NY, (n, 0, Y_CAP[0]), Y_RIGHT, Y_LEFT, 1,
        lambda m: stacked(m, tri_all), lambda m: stacked(m, ones_all),
    )
    hist = pick(line, my, NY)
    start = dot32(hist, tri_all)
    last = jnp.where(hist > 0, start + hist - 1, MERGE)
    y_lists = placed(last, pick(y_slot, my, NY), hist > 0)
    finals = jnp.zeros((1, n), jnp.int32)
    for hop in range(1, NY):
        source = (my + NY - hop) % NY
        there = jnp.where(pick(line, source, NY) > 0, pick(y_addr, source, NY), 0)
        finals = jnp.where(lane8[:1] // seg == hop, there, finals)

    arrived = here & (home8 == mx)
    wanted8 = (dy8 + NY - my) % NY * LB + spare8
    y_src = jnp.zeros((1, n), jnp.int32)
    y_first = jnp.zeros((1, n), jnp.int32)
    ahead = start
    for z in range(NZ):
        valid = arrived[z : z + 1]
        hot = ones_where(jnp.broadcast_to(jnp.where(valid, wanted8[z : z + 1], n), wide) == low)
        inner = dot32(hot, tri_all)
        rank = jnp.sum(jnp.where(hot > 0, inner, 0), axis=0, keepdims=True)
        seat = dot32(ahead, hot) + rank
        first = ones_where(seat == dot32(start, hot))
        y_src = y_src + placed(x_addr[z : z + 1], seat, valid)
        y_first = y_first + placed(first, seat, valid)
        ahead = ahead + dot32(jnp.ones((1, n), jnp.bfloat16), hot, True)
    flag = jnp.max(bad.astype(jnp.float32), axis=(0, 1), keepdims=True).astype(jnp.int32)
    flag = jnp.broadcast_to(flag, (1, n))
    x_tab = jnp.minimum(x_tab, Z_SLOTS - 1)
    y_src = jnp.minimum(y_src, X_SLOTS - 1)
    last = jnp.minimum(last, MERGE)
    y_lists = jnp.minimum(y_lists, MERGE)
    finals = jnp.minimum(finals, Y_SLOTS - 1)
    return jnp.concatenate([x_tab, y_src, y_first, last, y_lists, finals, flag, flag], axis=0)


def messages(r, feats, weight, msgs):
    step, per = 256, feats.shape[0] // TILE
    for s in range(feats.shape[0] // step):
        m = jnp.dot(
            feats[s * step : (s + 1) * step, :], weight[r], preferred_element_type=jnp.float32
        ).astype(jnp.bfloat16)
        spot = r * per + s * (step // TILE)
        msgs[spot : spot + step // TILE] = m.reshape(step // TILE, TILE, m.shape[1])


def partial_of(p, picks, tiles, msgs):
    kt = tiles.shape[2] // TILE
    rhs = jnp.concatenate([msgs[picks[p * kt + k]] for k in range(kt)], axis=0)
    return jnp.dot(tiles[p], rhs, preferred_element_type=jnp.float32).astype(jnp.bfloat16)


def partials_kernel(picks, feats, weight, tiles, out, msgs):
    for r in range(weight.shape[0]):
        messages(r, feats, weight, msgs)

    def one(p, carry):
        out[p] = partial_of(p, picks, tiles, msgs)
        return carry

    lax.fori_loop(0, tiles.shape[0], one, 0)


ORDER = (
    0, 1, 500, 10, 11, 20, 21, 30, 2, 3, 40, 100, 31, 12, 41, 110, 13, 101, 120, 22,
    200, 23, 32, 111, 4, 33, 42, 5, 102, 121, 201, 210, 14, 43, 103, 15, 211, 112, 24, 220,
    300, 221, 25, 301, 122, 34, 6, 113, 310, 202, 44, 104, 35, 320, 123, 16, 45, 105, 7, 114,
    212, 26, 17, 115, 222, 203, 311, 302, 36, 400, 124, 204, 27, 46, 106, 213, 125, 37, 205, 47,
    107, 214, 321, 215, 116, 223, 224, 117, 303, 225, 126, 206, 401, 304, 127, 207, 312, 305, 322, 314,
    216, 315, 313, 402, 217, 324, 325, 226, 306, 323, 227, 307, 403, 404, 316, 405, 317, 326, 327, 406,
    407,
)


def schedule():
    return [("zxyrgt"[n // 100], n // 10 % 10, n % 10) for n in ORDER]


def within(index, size):
    return jnp.minimum(jnp.maximum(index, 0), size - 1)


def layer_kernel(order, *refs):
    it = iter(refs)
    picks, key, feats, weight, tiles, counts, mix, bias, out, flag = [next(it) for _ in range(10)]
    msgs, part, keys, z_tab_vec, z_tab_all, tab_vec, tab_all = [next(it) for _ in range(7)]
    zs = [next(it) for _ in range(CHUNKS)]
    zb = [next(it) for _ in range(CHUNKS)]
    xs = [next(it) for _ in range(CHUNKS)]
    xb = [next(it) for _ in range(CHUNKS)]
    ys = [next(it) for _ in range(CHUNKS)]
    yb = [next(it) for _ in range(CHUNKS)]
    rs = [next(it) for _ in range(CHUNKS)]
    rb = [next(it) for _ in range(CHUNKS)]
    ag = [next(it) for _ in range(CHUNKS)]
    stage, total, degree = next(it), next(it), next(it)
    z_sems, x_sems, y_sems, r_sems = [(next(it), next(it)) for _ in range(4)]
    h_send, h_recv, k_send, k_recv, tab_sem = [next(it) for _ in range(5)]
    z_tab, tab = z_tab_all.at[0], tab_all

    me, half = lax.axis_index("rows"), lax.axis_index("half")
    mz, mx, my = me // (NX * NY), (me // NY) % NX, me % NY

    def at(z, x, y):
        return {"rows": (z % NZ) * (NX * NY) + (x % NX) * NY + y % NY}

    zp, zm = at(mz + 1, mx, my), at(mz + NZ - 1, mx, my)
    xp, xm = at(mz, mx + 1, my), at(mz, mx + NX - 1, my)
    yp, ym = at(mz, mx, my + 1), at(mz, mx, my + NY - 1)
    other = {"half": 1 - half}
    hops = [at(mz + k, mx, my) for k in range(1, NZ)]
    hops += [at(mz, mx + k, my) for k in range(1, NX)]
    hops += [at(mz, mx, my + k) for k in range(1, NY)]

    barrier = pltpu.get_barrier_semaphore()
    for device in hops + [other]:
        pl.semaphore_signal(barrier, inc=1, device_id=device, device_id_type=MESH)

    def key_copies(first, n, src, dst):
        return [
            copy(src, dst, k_send.at[i], k_recv.at[i], hops[i]) for i in range(first, first + n)
        ]

    def copy(src, dst, send, recv, device):
        return pltpu.make_async_remote_copy(
            src_ref=src, dst_ref=dst, send_sem=send, recv_sem=recv,
            device_id=device, device_id_type=MESH,
        )

    along_z = key_copies(0, NZ - 1, key, keys.at[my, mx, mz])
    along_x = key_copies(NZ - 1, NX - 1, keys.at[my, mx], keys.at[my, mx])
    along_y = key_copies(NZ + NX - 2, NY - 1, keys.at[my], keys.at[my])

    def begin(items):
        for item in items:
            item.start()

    def landed(items):
        for item in items:
            item.wait_recv()

    keys[my, mx, mz] = key[...]
    z_tab_vec[...] = tables(key[...], me, True)
    messages(0, feats, weight, msgs)
    pl.semaphore_wait(barrier, len(hops) + 1)
    begin(along_z)
    z_tab_copy = pltpu.make_async_copy(z_tab_vec, z_tab_all, tab_sem.at[0])
    z_tab_copy.start()
    for r in range(1, weight.shape[0]):
        messages(r, feats, weight, msgs)

    def one(p, carry):
        v = partial_of(p, picks, tiles, msgs)
        for i in range(ROW_CHUNKS):
            for j in range(COL_CHUNKS):
                part[i * COL_CHUNKS + j, p] = v[
                    i * HEIGHT : (i + 1) * HEIGHT, j * COLS : (j + 1) * COLS
                ]
        return carry

    parts = tiles.shape[0]
    lax.fori_loop(0, parts // 4, one, 0)
    landed(along_z)
    begin(along_x)
    lax.fori_loop(parts // 4, 5 * parts // 8, one, 0)
    landed(along_x)
    begin(along_y)
    lax.fori_loop(5 * parts // 8, parts, one, 0)
    z_tab_copy.wait()

    def gather(dst, base, read, entry, n):
        def body(j, carry):
            dst[base + j] = read(entry(j))
            return carry

        lax.fori_loop(0, n, body, 0, unroll=4)

    def hop_copies(sent, held, sems, forward, backward, caps, right, left):
        def copies(c, k):
            n = caps[k]
            result = []
            for side, device, base in ((0, forward, right), (1, backward, left)):
                if k == 0:
                    src = sent[c].at[pl.ds(side * n, n)]
                else:
                    src = held[c].at[pl.ds(base[k - 1], n)]
                dst = held[c].at[pl.ds(base[k], n)]
                result.append(copy(src, dst, sems[0].at[c, k, side], sems[1].at[c, k, side], device))
            return result

        return copies, len(caps)

    def h_copy(c):
        return copy(ag[c].at[half], ag[c].at[half], h_send.at[c], h_recv.at[c], other)

    stage[MERGE] = jnp.zeros(stage.shape[1:], stage.dtype)
    for c in range(CHUNKS):
        xb[c][0] = jnp.zeros(xb[c].shape[1:], xb[c].dtype)
        yb[c][0] = jnp.zeros(yb[c].shape[1:], yb[c].dtype)

    ring = {
        "z": hop_copies(zs, zb, z_sems, zp, zm, Z_CAP, Z_RIGHT, Z_LEFT),
        "x": hop_copies(xs, xb, x_sems, xp, xm, X_CAP, X_RIGHT, X_LEFT),
        "y": hop_copies(ys, yb, y_sems, yp, ym, Y_CAP, Y_RIGHT, Y_LEFT),
        "r": hop_copies(rs, rb, r_sems, xp, xm, (R_LIST, FAR), (0, 2 * R_LIST), (R_LIST, 2 * R_LIST + FAR)),
    }
    X_TAB, Y_SRC, Y_FIRST, LAST, LISTS, FINALS = range(6)

    for kind, k, c in order:
        row, col = c // COL_CHUNKS, c % COL_CHUNKS
        if kind == "t":
            landed(along_y)

            def add_up(y):
                def body(i, held):
                    return held + keys[y, i // NZ, i % NZ]

                return lax.fori_loop(0, NX * NZ, body, jnp.zeros((8, 128), jnp.int32), unroll=4)

            found = tables(jnp.concatenate([add_up(y) for y in range(NY)], axis=0), me)
            tab_vec[...] = found
            flag[...] = found
            tab_copy = pltpu.make_async_copy(tab_vec, tab_all, tab_sem.at[1])
            tab_copy.start()
            eye = iota((128, 128), 0) == iota((128, 128), 1)
            per = 128 // TILE
            for i in range(LB // per):
                one_row = jnp.broadcast_to(counts[i : i + 1].astype(jnp.float32), (128, 128))
                spread = jnp.dot(
                    jnp.where(eye, one_row, 0.0).astype(jnp.bfloat16),
                    jnp.ones((128, COLS), jnp.bfloat16),
                    preferred_element_type=jnp.float32,
                )
                degree[i * per : (i + 1) * per] = spread.reshape(per, TILE, COLS)
            tab_copy.wait()
        elif kind in ring and k > 0:
            copies, hops = ring[kind]
            for item in copies(c, k - 1):
                item.wait_recv()
            if k < hops:
                for item in copies(c, k):
                    item.start()
            elif kind == "r":

                def finish(base, first, n):
                    def body(i, carry):
                        b = first + i
                        v = rb[c][base + i].astype(jnp.float32)
                        v = v / degree[b, row * HEIGHT : (row + 1) * HEIGHT, :]
                        ag[c][half, b] = v.astype(jnp.bfloat16)
                        return carry

                    lax.fori_loop(0, n, body, 0, unroll=4)

                far = 2 * R_LIST
                finish(far + 2 * FAR, mx * GROUP, GROUP)
                finish(FAR, (mx + NX - 1) % NX * GROUP, GROUP)
                finish(R_LIST + FAR, (mx + 1) % NX * GROUP, GROUP)
                finish(far, (mx + 2) % NX * GROUP, GROUP)
                h_copy(c).start()
        elif kind == "z":
            read = lambda i: part[c, i]
            gather(zs[c], 0, read, lambda j: within(z_tab[Z_LOCAL + j], parts), 2 * Z_CAP[0])
            for item in ring["z"][0](c, 0):
                item.start()
            gather(zb[c], 0, read, lambda j: within(z_tab[j], parts), Z_LOCAL)
        elif kind == "x":
            read = lambda i: zb[c][i]
            gather(xs[c], 0, read, lambda j: within(tab[X_TAB, X_LOCAL + j], Z_SLOTS), 2 * X_CAP[0])
            for item in ring["x"][0](c, 0):
                item.start()
            gather(xb[c], 1, read, lambda j: within(tab[X_TAB, j], Z_SLOTS), X_LOCAL)
        elif kind == "y":

            def add(j, total_now):
                v = xb[c][within(tab[Y_SRC, j], X_SLOTS)].astype(jnp.float32)
                total_now = jnp.where(tab[Y_FIRST, j] > 0, v, total_now + v)
                stage[j] = total_now.astype(stage.dtype)
                return total_now

            lax.fori_loop(0, MERGE, add, jnp.zeros((HEIGHT, COLS), jnp.float32), unroll=4)
            read = lambda i: stage[i]
            gather(ys[c], 0, read, lambda j: within(tab[LISTS, j], MERGE + 1), 2 * Y_CAP[0])
            for item in ring["y"][0](c, 0):
                item.start()
            gather(yb[c], 1, read, lambda j: within(tab[LAST, j], MERGE + 1), LB)
        elif kind == "r":

            def collect(dst, base, hop, first, n):
                group = (mx + hop) % NX * GROUP + first

                def body(i, carry):
                    q = group + i
                    v = yb[c][1 + q].astype(jnp.float32)
                    for other_y in range(NY - 1):
                        v = v + yb[c][within(tab[FINALS, (other_y + 1) * LB + q], Y_SLOTS)].astype(jnp.float32)
                    dst[base + i] = v.astype(dst.dtype)
                    return carry

                lax.fori_loop(0, n, body, 0, unroll=4)

            collect(rs[c], 0, 2, 0, FAR)
            collect(rs[c], FAR, 1, 0, GROUP)
            collect(rs[c], R_LIST, 2, FAR, FAR)
            collect(rs[c], R_LIST + FAR, NX - 1, 0, GROUP)
            for item in ring["r"][0](c, 0):
                item.start()
            collect(rb[c], 2 * R_LIST + 2 * FAR, 0, 0, GROUP)
        else:
            h_copy(c).wait_recv()
            some = 8
            width = mix.shape[0] // 2
            w = jnp.concatenate(
                [
                    mix[col * COLS : (col + 1) * COLS, :],
                    mix[width + col * COLS : width + (col + 1) * COLS, :],
                ],
                axis=0,
            )

            def mixing(b, carry):
                blocks = pl.ds(b * some, some)
                a = jnp.concatenate(
                    [
                        ag[c][0, blocks].reshape(some * HEIGHT, COLS),
                        ag[c][1, blocks].reshape(some * HEIGHT, COLS),
                    ],
                    axis=1,
                )
                v = jnp.dot(a, w, preferred_element_type=jnp.float32)
                v = v.reshape(some, HEIGHT, v.shape[1])
                if col > 0:
                    v = v + total[blocks]
                if col < COL_CHUNKS - 1:
                    total[blocks] = v
                else:
                    v = jnp.maximum(v + bias[...][None], 0.0)
                    out[blocks, row * HEIGHT : (row + 1) * HEIGHT, :] = v.astype(out.dtype)
                return carry

            lax.fori_loop(0, LB // some, mixing, 0)

    for c in range(CHUNKS):
        for copies, hops in ring.values():
            for k in range(hops):
                for item in copies(c, k):
                    item.wait_send()
        h_copy(c).wait_send()
    for item in along_z + along_x + along_y:
        item.wait_send()


def vmem():
    return pl.BlockSpec(memory_space=pltpu.VMEM)


def smem():
    return pl.BlockSpec(memory_space=pltpu.SMEM)


def local(
    source_feats, rel_weight, tiles, src_blk, rel_id, owner, local_blk, in_degree, mix_weight, bias
):
    n_rows = lax.axis_size("rows")
    src_dev, half_w = source_feats.shape
    tile = tiles.shape[1]
    parts, per_row = src_blk.shape
    n_rel = rel_weight.shape[0]
    n_src_blocks = src_dev // tile
    n_local = in_degree.shape[0] // tile

    me = lax.axis_index("rows")
    spot_z = lax.broadcasted_iota(jnp.int32, (NZ, 128), 0) == me // (NX * NY)
    spot_x = lax.broadcasted_iota(jnp.int32, (NZ, 128), 1) // LB == (me // NY) % NX
    own = jnp.tile(owner[:, 0] * LB + local_blk, 128 // parts)
    key = jnp.where(spot_z & spot_x, own[None, :], 0)
    weight = rel_weight.reshape(n_rel, half_w, half_w)
    picks = (rel_id * n_src_blocks + src_blk).reshape(-1)
    n_hops = NZ + NX + NY - 3
    degree = in_degree.astype(jnp.float32)
    block = lambda n: [pltpu.VMEM((n, HEIGHT, COLS), jnp.bfloat16)] * CHUNKS
    dma = pltpu.SemaphoreType.DMA
    pair = lambda n: [dma((CHUNKS, n, 2)), dma((CHUNKS, n, 2))]
    out, flag = pl.pallas_call(
        functools.partial(layer_kernel, schedule()),
        out_shape=(
            jax.ShapeDtypeStruct((n_local, tile, half_w), jnp.bfloat16),
            jax.ShapeDtypeStruct((8, 128), jnp.int32),
        ),
        in_specs=[smem()] + [vmem()] * 7,
        out_specs=(vmem(), vmem()),
        scratch_shapes=[
            pltpu.VMEM((n_rel * n_src_blocks, tile, half_w), jnp.bfloat16),
            pltpu.VMEM((CHUNKS, parts, HEIGHT, COLS), jnp.bfloat16),
            pltpu.VMEM((NY, NX, NZ, 8, 128), jnp.int32),
            pltpu.VMEM((8, 128), jnp.int32),
            pltpu.SMEM((8, 128), jnp.int32),
            pltpu.VMEM((8, 128), jnp.int32),
            pltpu.SMEM((8, 128), jnp.int32),
        ]
        + block(2 * Z_CAP[0])
        + block(Z_SLOTS)
        + block(2 * X_CAP[0])
        + block(X_SLOTS)
        + block(2 * Y_CAP[0])
        + block(Y_SLOTS)
        + block(2 * R_LIST)
        + block(2 * R_LIST + 2 * FAR + GROUP)
        + [pltpu.VMEM((2, n_local, HEIGHT, COLS), jnp.bfloat16)] * CHUNKS
        + [
            pltpu.VMEM((MERGE + 1, HEIGHT, COLS), jnp.bfloat16),
            pltpu.VMEM((n_local, HEIGHT, half_w), jnp.float32),
            pltpu.VMEM((n_local, tile, COLS), jnp.float32),
        ]
        + pair(len(Z_CAP))
        + pair(len(X_CAP))
        + pair(len(Y_CAP))
        + pair(2)
        + [dma((CHUNKS,)), dma((CHUNKS,)), dma((n_hops,)), dma((n_hops,)), dma((2,))],
        compiler_params=pltpu.CompilerParams(
            collective_id=0, has_side_effects=True, vmem_limit_bytes=67043328
        ),
    )(picks, key, source_feats, weight, tiles, in_degree.reshape(-1, 128), mix_weight, bias[None, :])
    out = out.reshape(n_local * tile, half_w)

    def dense():
        partials = pl.pallas_call(
            partials_kernel,
            out_shape=jax.ShapeDtypeStruct((parts, tile, half_w), jnp.bfloat16),
            in_specs=[smem(), vmem(), vmem(), vmem()],
            out_specs=vmem(),
            scratch_shapes=[pltpu.VMEM((n_rel * n_src_blocks, tile, half_w), jnp.bfloat16)],
        )(picks, source_feats, weight, tiles).reshape(parts, tile * half_w)
        capacity = max(2, 2 * parts // n_rows)
        target_dev = owner[:, 0]
        positions = jnp.arange(parts, dtype=jnp.int32)
        earlier = (target_dev[:, None] == target_dev[None, :]) & (
            positions[None, :] < positions[:, None]
        )
        rank = jnp.sum(earlier.astype(jnp.int32), axis=1)
        slot = target_dev * capacity + rank
        slot_ids = jnp.arange(n_rows * capacity, dtype=jnp.int32)
        placing = slot_ids[:, None] == slot[None, :]
        outgoing = jnp.dot(
            placing.astype(jnp.bfloat16), partials, preferred_element_type=jnp.float32
        ).astype(jnp.bfloat16)
        out_ids = jnp.sum(jnp.where(placing, local_blk[None, :] + 1, 0), axis=1) - 1
        block_index = jnp.arange(n_local, dtype=jnp.int32)
        arrived = lax.all_to_all(outgoing, "rows", split_axis=0, concat_axis=0, tiled=True)
        arrived_ids = lax.all_to_all(out_ids, "rows", split_axis=0, concat_axis=0, tiled=True)
        selector = (arrived_ids[None, :] == block_index[:, None]).astype(jnp.bfloat16)
        summed = jnp.dot(selector, arrived, preferred_element_type=jnp.float32)
        summed = summed.reshape(n_local * tile, half_w)
        agg = (summed / degree[:, None]).astype(jnp.bfloat16)
        theirs = lax.ppermute(agg, "half", [(0, 1), (1, 0)])
        half = lax.axis_index("half")
        w_mine = lax.dynamic_slice_in_dim(mix_weight, half * half_w, half_w, 0)
        w_theirs = lax.dynamic_slice_in_dim(mix_weight, (1 - half) * half_w, half_w, 0)
        mixed = jnp.dot(
            jnp.concatenate([agg, theirs], axis=1),
            jnp.concatenate([w_mine, w_theirs], axis=0),
            preferred_element_type=jnp.float32,
        )
        return jax.nn.relu(mixed + bias).astype(jnp.bfloat16)

    return lax.cond(flag[6, 0] > 0, dense, lambda: out)


def solution(mesh):
    placed = (
        P("rows", "half"),
        P(None, "half", None, None),
        P("rows", None, None),
        P("rows", None),
        P("rows", None),
        P("rows", None),
        P("rows"),
        P("rows"),
        P(None, "half"),
        P("half"),
    )
    return jax.shard_map(
        local, mesh=mesh, in_specs=placed, out_specs=P("rows", "half"), check_vma=False
    )
```

```python
import functools

import jax
import jax.numpy as jnp
from jax import lax
from jax.experimental import pallas as pl
from jax.experimental.pallas import tpu as pltpu
from jax.sharding import PartitionSpec as P

MESH = pl.DeviceIdType.MESH
NZ, NX, NY = 8, 4, 4
ROWS = NZ * NX * NY
TILE = 64
REL = 3
LB = 32

Z_LOCAL, Z_CAP = 12, (24, 20, 14, 6)
X_LOCAL, X_CAP = 32, (34, 15)
MERGE = 96
Y_CAP = (26, 12)
GROUP = LB // NX
FAR = GROUP // 2
R_LIST = GROUP + FAR

COLS = 128
HEIGHT = 32
COL_CHUNKS = 4
ROW_CHUNKS = TILE // HEIGHT
CHUNKS = COL_CHUNKS * ROW_CHUNKS


def bases(local, caps, start):
    right, left, at = [], [], start + local
    for cap in caps:
        right.append(at)
        at += cap
    for cap in caps:
        left.append(at)
        at += cap
    return right, left, at


Z_RIGHT, Z_LEFT, Z_SLOTS = bases(Z_LOCAL, Z_CAP, 0)
X_RIGHT, X_LEFT, X_SLOTS = bases(X_LOCAL, X_CAP, 1)
Y_RIGHT, Y_LEFT, Y_SLOTS = bases(LB, Y_CAP, 1)


def ones_where(mask):
    return jnp.where(mask, 1.0, 0.0).astype(jnp.bfloat16)


def iota(shape, axis):
    return lax.broadcasted_iota(jnp.int32, shape, axis)


def dot32(a, b, transposed=False):
    dims = (((1,), (1 if transposed else 0,)), ((), ()))
    v = lax.dot_general(
        a.astype(jnp.bfloat16), b.astype(jnp.bfloat16), dims, preferred_element_type=jnp.float32
    )
    return v.astype(jnp.int32)


def tables(k, me, first_only=False):
    mz, mx, my = me // (NX * NY), (me // NY) % NX, me % NY
    n, seg = 128, LB
    wide = (n, n)
    low, col = iota(wide, 0), iota(wide, 1)
    same = (low // seg) == (col // seg)
    tri_all = ones_where(low < col)
    tri_seg = ones_where((low < col) & same)
    sum_seg = ones_where(same)
    shape = k.shape
    lane, row = iota(shape, 1), iota(shape, 0)
    owner, block = k // LB, k % LB
    dz, dy = owner // (NX * NY), owner % NY
    home, spare = block // GROUP, (owner // NY) % NX * GROUP + block % GROUP
    sz, sy, sx, p = row % NZ, row // NZ, lane // seg, lane % seg

    def number(mask):
        return jnp.where(mask, 1, 0)

    def listed(delta, ring, starts, right_base, left_base, local_base, before, total):
        half = ring // 2
        odd = before([delta == half])[0] % 2
        to_right = ((delta >= 1) & (delta < half)) | ((delta == half) & (odd == 0))
        to_left = ((delta > half) & (delta < ring)) | ((delta == half) & (odd == 1))
        dist = jnp.where(delta <= half, delta, ring - delta)
        masks = [delta == 0]
        masks += [to_right & (dist == h) for h in range(1, half + 1)]
        masks += [to_left & (dist == h) for h in range(1, half + 1)]
        ranks, totals = before(masks), total(masks)
        address = jnp.where(masks[0], local_base + ranks[0], 0)
        slot = jnp.where(masks[0], starts[0] + ranks[0], n)
        worst = []
        for side, base in ((0, right_base), (1, left_base)):
            farther = jnp.zeros_like(totals[0])
            for h in range(half, 0, -1):
                at = 1 + side * half + h - 1
                address = jnp.where(masks[at], base[h - 1] + farther + ranks[at], address)
                slot = jnp.where(masks[at], starts[1 + side] + farther + ranks[at], slot)
                farther = farther + totals[at]
                worst.append((h - 1, farther))
        return address, slot, totals[0], worst

    def stacked(masks, matrix):
        v = dot32(jnp.concatenate([ones_where(m) for m in masks], axis=0), matrix)
        rows = masks[0].shape[0]
        return [v[i * rows : (i + 1) * rows] for i in range(len(masks))]

    def overflow(kept, local, worst, caps):
        bad = number(kept > local)
        for h, count in worst:
            bad = bad | number(count > caps[h])
        return bad

    z_addr, z_slot, z_kept, z_worst = listed(
        (dz + NZ - sz) % NZ, NZ, (0, Z_LOCAL, Z_LOCAL + Z_CAP[0]), Z_RIGHT, Z_LEFT, 0,
        lambda m: stacked(m, tri_seg), lambda m: stacked(m, sum_seg),
    )
    bad = overflow(z_kept, Z_LOCAL, z_worst, Z_CAP)

    def placed(values, slots, valid):
        hit = ones_where(jnp.broadcast_to(jnp.where(valid, slots, n), wide) == low)
        return dot32(values, hit, True)

    def pick(a, index, count):
        total = jnp.zeros_like(a[:1])
        for i in range(count):
            total = jnp.where(index == i, a[i : i + 1], total)
        return total

    def pick_y(a):
        total = jnp.zeros_like(a[:NZ])
        for i in range(NY):
            total = jnp.where(my == i, a[i * NZ : (i + 1) * NZ], total)
        return total

    lane8 = iota((NZ, n), 1)
    own = pick(z_slot if first_only else pick_y(z_slot), mz, NZ)
    if first_only:
        z_tab = placed(lane8[:1] % seg, own, lane8[:1] // seg == mx)
        return jnp.broadcast_to(jnp.minimum(z_tab, seg - 1), (NZ, n))

    def before_x(masks):
        inner, whole = stacked(masks, tri_seg), stacked(masks, sum_seg)
        r, c = iota((NZ, NZ), 0), iota((NZ, NZ), 1)
        lower = ones_where(c < r)
        groups = masks[0].shape[0] // NZ
        outer = [
            jnp.concatenate([dot32(lower, w[g * NZ : (g + 1) * NZ]) for g in range(groups)], axis=0)
            for w in whole
        ]
        return [a + b for a, b in zip(inner, outer)]

    def total_x(masks):
        whole = stacked(masks, sum_seg)
        groups = masks[0].shape[0] // NZ
        return [
            jnp.concatenate(
                [
                    jnp.broadcast_to(
                        jnp.sum(w[g * NZ : (g + 1) * NZ], axis=0, keepdims=True), (NZ, n)
                    )
                    for g in range(groups)
                ],
                axis=0,
            )
            for w in whole
        ]

    dz8, home8, dy8, spare8 = pick_y(dz), pick_y(home), pick_y(dy), pick_y(spare)
    here = dz8 == mz
    x_addr, x_slot, _, _ = listed(
        jnp.where(here, (home8 + NX - lane8 // seg) % NX, NX), NX,
        (0, X_LOCAL, X_LOCAL + X_CAP[0]), X_RIGHT, X_LEFT, 1, before_x, total_x,
    )
    z_addr8 = pick_y(z_addr)
    x_tab = jnp.zeros((1, n), jnp.int32)
    for z in range(NZ):
        x_tab = x_tab + placed(
            z_addr8[z : z + 1], x_slot[z : z + 1], here[z : z + 1] & (lane8[:1] // seg == mx)
        )
    for z in range(NZ):
        deltas = [(dz == z) & ((home + NX - sx) % NX == d) for d in range(NX)]
        kept, right, tied, left = total_x(deltas)
        near, far = tied // 2, (tied + 1) // 2
        bad = bad | overflow(kept, X_LOCAL, [(1, far), (0, far + right), (0, near + left)], X_CAP)

    spots = dz * NX + home
    wanted = (dy + NY - sy) % NY * LB + spare
    hists = []
    holder = iota((NZ * NX, n), 0)
    for y in range(NY):
        total = jnp.zeros((NZ * NX, n), jnp.int32)
        for z in range(NZ):
            r = y * NZ + z
            holds = ones_where(jnp.broadcast_to(spots[r : r + 1], (NZ * NX, n)) == holder)
            wants = ones_where(jnp.broadcast_to(wanted[r : r + 1], wide) == low)
            total = total + dot32(holds, wants, True)
        hists.append(total)
        count = jnp.sum(total, axis=1, keepdims=True)
        bad = bad | number(jnp.broadcast_to(count, total.shape) > MERGE)
        present = dot32(ones_where(total > 0), sum_seg)
        group = iota(total.shape, 1) // seg
        tied = present
        bad = bad | number((group == 1) & (present > Y_CAP[0]))
        bad = bad | number((group == 3) & (present > Y_CAP[0]))
        bad = bad | number((group == 2) & ((present + 1) // 2 > Y_CAP[1]))
        ties = ones_where((total > 0) & (group == 2))
        every = dot32(ties, jnp.ones(wide, jnp.bfloat16))
        bad = bad | number((group == 1) & (present + (every + 1) // 2 > Y_CAP[0]))
        bad = bad | number((group == 3) & (present + every // 2 > Y_CAP[0]))
    index = mz * NX + mx
    lines = []
    for y in range(NY):
        mine = iota((NZ * NX, n), 0) == index
        lines.append(jnp.sum(jnp.where(mine, hists[y], 0), axis=0, keepdims=True))
    pad = [jnp.zeros((1, n), jnp.int32)] * (NZ - NY)
    line = jnp.concatenate(lines + pad, axis=0)
    ones_all = jnp.ones(wide, jnp.bfloat16)
    y_addr, y_slot, _, _ = listed(
        jnp.where(line > 0, lane8 // seg, NY), NY, (n, 0, Y_CAP[0]), Y_RIGHT, Y_LEFT, 1,
        lambda m: stacked(m, tri_all), lambda m: stacked(m, ones_all),
    )
    hist = pick(line, my, NY)
    start = dot32(hist, tri_all)
    last = jnp.where(hist > 0, start + hist - 1, MERGE)
    y_lists = placed(last, pick(y_slot, my, NY), hist > 0)
    finals = jnp.zeros((1, n), jnp.int32)
    for hop in range(1, NY):
        source = (my + NY - hop) % NY
        there = jnp.where(pick(line, source, NY) > 0, pick(y_addr, source, NY), 0)
        finals = jnp.where(lane8[:1] // seg == hop, there, finals)

    arrived = here & (home8 == mx)
    wanted8 = (dy8 + NY - my) % NY * LB + spare8
    y_src = jnp.zeros((1, n), jnp.int32)
    y_first = jnp.zeros((1, n), jnp.int32)
    ahead = start
    for z in range(NZ):
        valid = arrived[z : z + 1]
        hot = ones_where(jnp.broadcast_to(jnp.where(valid, wanted8[z : z + 1], n), wide) == low)
        inner = dot32(hot, tri_all)
        rank = jnp.sum(jnp.where(hot > 0, inner, 0), axis=0, keepdims=True)
        seat = dot32(ahead, hot) + rank
        first = ones_where(seat == dot32(start, hot))
        y_src = y_src + placed(x_addr[z : z + 1], seat, valid)
        y_first = y_first + placed(first, seat, valid)
        ahead = ahead + dot32(jnp.ones((1, n), jnp.bfloat16), hot, True)
    flag = jnp.max(bad.astype(jnp.float32), axis=(0, 1), keepdims=True).astype(jnp.int32)
    flag = jnp.broadcast_to(flag, (1, n))
    x_tab = jnp.minimum(x_tab, Z_SLOTS - 1)
    y_src = jnp.minimum(y_src, X_SLOTS - 1)
    last = jnp.minimum(last, MERGE)
    y_lists = jnp.minimum(y_lists, MERGE)
    finals = jnp.minimum(finals, Y_SLOTS - 1)
    return jnp.concatenate([x_tab, y_src, y_first, last, y_lists, finals, flag, flag], axis=0)


def messages(r, feats, weight, msgs):
    step, per = 256, feats.shape[0] // TILE
    for s in range(feats.shape[0] // step):
        m = jnp.dot(
            feats[s * step : (s + 1) * step, :], weight[r], preferred_element_type=jnp.float32
        ).astype(jnp.bfloat16)
        spot = r * per + s * (step // TILE)
        msgs[spot : spot + step // TILE] = m.reshape(step // TILE, TILE, m.shape[1])


def partial_of(p, rel, src, tiles, msgs):
    per = msgs.shape[0] // REL
    kt = tiles.shape[2] // TILE
    rhs = jnp.concatenate([msgs[within(rel[k, p] * per + src[k, p], REL * per)] for k in range(kt)], axis=0)
    return jnp.dot(tiles[p], rhs, preferred_element_type=jnp.float32).astype(jnp.bfloat16)


def partials_kernel(rel, src, feats, weight, tiles, out, msgs):
    for r in range(weight.shape[0]):
        messages(r, feats, weight, msgs)

    def one(p, carry):
        out[p] = partial_of(p, rel, src, tiles, msgs)
        return carry

    lax.fori_loop(0, tiles.shape[0], one, 0)


ORDER = (
    0, 1, 500, 10, 11, 20, 21, 30, 2, 3, 40, 100, 31, 12, 41, 110, 13, 101, 120, 22,
    200, 23, 32, 111, 4, 33, 42, 5, 102, 121, 201, 210, 14, 43, 103, 15, 211, 112, 24, 220,
    300, 221, 25, 301, 122, 34, 6, 113, 310, 202, 44, 104, 35, 320, 123, 16, 45, 105, 7, 114,
    212, 26, 17, 115, 222, 203, 311, 302, 36, 400, 124, 204, 27, 46, 106, 213, 125, 37, 205, 47,
    107, 214, 321, 215, 116, 223, 224, 117, 303, 225, 126, 206, 401, 304, 127, 207, 312, 305, 322, 314,
    216, 315, 313, 402, 217, 324, 325, 226, 306, 323, 227, 307, 403, 404, 316, 405, 317, 326, 327, 406,
    407,
)


def schedule():
    return [("zxyrgt"[n // 100], n // 10 % 10, n % 10) for n in ORDER]


def within(index, size):
    return jnp.minimum(jnp.maximum(index, 0), size - 1)


def layer_kernel(order, *refs):
    it = iter(refs)
    rel, src, key, feats, weight, tiles, counts, mix, bias, out, flag = [next(it) for _ in range(11)]
    msgs, part, keys, z_tab_vec, z_tab_all, tab_vec, tab_all = [next(it) for _ in range(7)]
    zs = [next(it) for _ in range(CHUNKS)]
    zb = [next(it) for _ in range(CHUNKS)]
    xs = [next(it) for _ in range(CHUNKS)]
    xb = [next(it) for _ in range(CHUNKS)]
    ys = [next(it) for _ in range(CHUNKS)]
    yb = [next(it) for _ in range(CHUNKS)]
    rs = [next(it) for _ in range(CHUNKS)]
    rb = [next(it) for _ in range(CHUNKS)]
    ag = [next(it) for _ in range(CHUNKS)]
    stage, total, degree = next(it), next(it), next(it)
    z_sems, x_sems, y_sems, r_sems = [(next(it), next(it)) for _ in range(4)]
    h_send, h_recv, k_send, k_recv, tab_sem = [next(it) for _ in range(5)]
    z_tab, tab = z_tab_all.at[0], tab_all

    me, half = lax.axis_index("rows"), lax.axis_index("half")
    mz, mx, my = me // (NX * NY), (me // NY) % NX, me % NY

    def at(z, x, y):
        return {"rows": (z % NZ) * (NX * NY) + (x % NX) * NY + y % NY}

    zp, zm = at(mz + 1, mx, my), at(mz + NZ - 1, mx, my)
    xp, xm = at(mz, mx + 1, my), at(mz, mx + NX - 1, my)
    yp, ym = at(mz, mx, my + 1), at(mz, mx, my + NY - 1)
    other = {"half": 1 - half}
    hops = [at(mz + k, mx, my) for k in range(1, NZ)]
    hops += [at(mz, mx + k, my) for k in range(1, NX)]
    hops += [at(mz, mx, my + k) for k in range(1, NY)]

    barrier = pltpu.get_barrier_semaphore()
    for device in hops + [other]:
        pl.semaphore_signal(barrier, inc=1, device_id=device, device_id_type=MESH)

    def key_copies(first, n, src, dst):
        return [
            copy(src, dst, k_send.at[i], k_recv.at[i], hops[i]) for i in range(first, first + n)
        ]

    def copy(src, dst, send, recv, device):
        return pltpu.make_async_remote_copy(
            src_ref=src, dst_ref=dst, send_sem=send, recv_sem=recv,
            device_id=device, device_id_type=MESH,
        )

    along_z = key_copies(0, NZ - 1, key, keys.at[my, mx, mz])
    along_x = key_copies(NZ - 1, NX - 1, keys.at[my, mx], keys.at[my, mx])
    along_y = key_copies(NZ + NX - 2, NY - 1, keys.at[my], keys.at[my])

    def begin(items):
        for item in items:
            item.start()

    def landed(items):
        for item in items:
            item.wait_recv()

    keys[my, mx, mz] = key[...]
    z_tab_vec[...] = tables(key[...], me, True)
    messages(0, feats, weight, msgs)
    pl.semaphore_wait(barrier, len(hops) + 1)
    begin(along_z)
    z_tab_copy = pltpu.make_async_copy(z_tab_vec, z_tab_all, tab_sem.at[0])
    z_tab_copy.start()
    for r in range(1, weight.shape[0]):
        messages(r, feats, weight, msgs)

    def one(p, carry):
        v = partial_of(p, rel, src, tiles, msgs)
        for i in range(ROW_CHUNKS):
            for j in range(COL_CHUNKS):
                part[i * COL_CHUNKS + j, p] = v[
                    i * HEIGHT : (i + 1) * HEIGHT, j * COLS : (j + 1) * COLS
                ]
        return carry

    parts = tiles.shape[0]
    lax.fori_loop(0, parts // 4, one, 0)
    landed(along_z)
    begin(along_x)
    lax.fori_loop(parts // 4, 5 * parts // 8, one, 0)
    landed(along_x)
    begin(along_y)
    lax.fori_loop(5 * parts // 8, parts, one, 0)
    z_tab_copy.wait()

    def gather(dst, base, read, entry, n):
        def body(j, carry):
            dst[base + j] = read(entry(j))
            return carry

        lax.fori_loop(0, n, body, 0, unroll=4)

    def hop_copies(sent, held, sems, forward, backward, caps, right, left):
        def copies(c, k):
            n = caps[k]
            result = []
            for side, device, base in ((0, forward, right), (1, backward, left)):
                if k == 0:
                    src = sent[c].at[pl.ds(side * n, n)]
                else:
                    src = held[c].at[pl.ds(base[k - 1], n)]
                dst = held[c].at[pl.ds(base[k], n)]
                result.append(copy(src, dst, sems[0].at[c, k, side], sems[1].at[c, k, side], device))
            return result

        return copies, len(caps)

    def h_copy(c):
        return copy(ag[c].at[half], ag[c].at[half], h_send.at[c], h_recv.at[c], other)

    stage[MERGE] = jnp.zeros(stage.shape[1:], stage.dtype)
    for c in range(CHUNKS):
        xb[c][0] = jnp.zeros(xb[c].shape[1:], xb[c].dtype)
        yb[c][0] = jnp.zeros(yb[c].shape[1:], yb[c].dtype)

    ring = {
        "z": hop_copies(zs, zb, z_sems, zp, zm, Z_CAP, Z_RIGHT, Z_LEFT),
        "x": hop_copies(xs, xb, x_sems, xp, xm, X_CAP, X_RIGHT, X_LEFT),
        "y": hop_copies(ys, yb, y_sems, yp, ym, Y_CAP, Y_RIGHT, Y_LEFT),
        "r": hop_copies(rs, rb, r_sems, xp, xm, (R_LIST, FAR), (0, 2 * R_LIST), (R_LIST, 2 * R_LIST + FAR)),
    }
    X_TAB, Y_SRC, Y_FIRST, LAST, LISTS, FINALS = range(6)

    for kind, k, c in order:
        row, col = c // COL_CHUNKS, c % COL_CHUNKS
        if kind == "t":
            landed(along_y)

            def add_up(y):
                def body(i, held):
                    return held + keys[y, i // NZ, i % NZ]

                return lax.fori_loop(0, NX * NZ, body, jnp.zeros((8, 128), jnp.int32), unroll=4)

            found = tables(jnp.concatenate([add_up(y) for y in range(NY)], axis=0), me)
            tab_vec[...] = found
            flag[0, 0] = jnp.max(found[6:7].astype(jnp.float32)).astype(jnp.int32)
            tab_copy = pltpu.make_async_copy(tab_vec, tab_all, tab_sem.at[1])
            tab_copy.start()
            eye = iota((128, 128), 0) == iota((128, 128), 1)
            per = 128 // TILE
            for i in range(LB // per):
                one_row = jnp.broadcast_to(counts[i : i + 1].astype(jnp.float32), (128, 128))
                spread = jnp.dot(
                    jnp.where(eye, one_row, 0.0).astype(jnp.bfloat16),
                    jnp.ones((128, COLS), jnp.bfloat16),
                    preferred_element_type=jnp.float32,
                )
                degree[i * per : (i + 1) * per] = spread.reshape(per, TILE, COLS)
            tab_copy.wait()
        elif kind in ring and k > 0:
            copies, hops = ring[kind]
            for item in copies(c, k - 1):
                item.wait_recv()
            if k < hops:
                for item in copies(c, k):
                    item.start()
            elif kind == "r":

                def finish(base, first, n):
                    def body(i, carry):
                        b = first + i
                        v = rb[c][base + i].astype(jnp.float32)
                        v = v / degree[b, row * HEIGHT : (row + 1) * HEIGHT, :]
                        ag[c][half, b] = v.astype(jnp.bfloat16)
                        return carry

                    lax.fori_loop(0, n, body, 0, unroll=4)

                far = 2 * R_LIST
                finish(far + 2 * FAR, mx * GROUP, GROUP)
                finish(FAR, (mx + NX - 1) % NX * GROUP, GROUP)
                finish(R_LIST + FAR, (mx + 1) % NX * GROUP, GROUP)
                finish(far, (mx + 2) % NX * GROUP, GROUP)
                h_copy(c).start()
        elif kind == "z":
            read = lambda i: part[c, i]
            gather(zs[c], 0, read, lambda j: within(z_tab[Z_LOCAL + j], parts), 2 * Z_CAP[0])
            for item in ring["z"][0](c, 0):
                item.start()
            gather(zb[c], 0, read, lambda j: within(z_tab[j], parts), Z_LOCAL)
        elif kind == "x":
            read = lambda i: zb[c][i]
            gather(xs[c], 0, read, lambda j: within(tab[X_TAB, X_LOCAL + j], Z_SLOTS), 2 * X_CAP[0])
            for item in ring["x"][0](c, 0):
                item.start()
            gather(xb[c], 1, read, lambda j: within(tab[X_TAB, j], Z_SLOTS), X_LOCAL)
        elif kind == "y":

            def add(j, total_now):
                v = xb[c][within(tab[Y_SRC, j], X_SLOTS)].astype(jnp.float32)
                total_now = jnp.where(tab[Y_FIRST, j] > 0, v, total_now + v)
                stage[j] = total_now.astype(stage.dtype)
                return total_now

            lax.fori_loop(0, MERGE, add, jnp.zeros((HEIGHT, COLS), jnp.float32), unroll=4)
            read = lambda i: stage[i]
            gather(ys[c], 0, read, lambda j: within(tab[LISTS, j], MERGE + 1), 2 * Y_CAP[0])
            for item in ring["y"][0](c, 0):
                item.start()
            gather(yb[c], 1, read, lambda j: within(tab[LAST, j], MERGE + 1), LB)
        elif kind == "r":

            def collect(dst, base, hop, first, n):
                group = (mx + hop) % NX * GROUP + first

                def body(i, carry):
                    q = group + i
                    v = yb[c][1 + q].astype(jnp.float32)
                    for other_y in range(NY - 1):
                        v = v + yb[c][within(tab[FINALS, (other_y + 1) * LB + q], Y_SLOTS)].astype(jnp.float32)
                    dst[base + i] = v.astype(dst.dtype)
                    return carry

                lax.fori_loop(0, n, body, 0, unroll=4)

            collect(rs[c], 0, 2, 0, FAR)
            collect(rs[c], FAR, 1, 0, GROUP)
            collect(rs[c], R_LIST, 2, FAR, FAR)
            collect(rs[c], R_LIST + FAR, NX - 1, 0, GROUP)
            for item in ring["r"][0](c, 0):
                item.start()
            collect(rb[c], 2 * R_LIST + 2 * FAR, 0, 0, GROUP)
        else:
            h_copy(c).wait_recv()
            some = 8
            width = mix.shape[0] // 2
            w = jnp.concatenate(
                [
                    mix[col * COLS : (col + 1) * COLS, :],
                    mix[width + col * COLS : width + (col + 1) * COLS, :],
                ],
                axis=0,
            )

            def mixing(b, carry):
                blocks = pl.ds(b * some, some)
                a = jnp.concatenate(
                    [
                        ag[c][0, blocks].reshape(some * HEIGHT, COLS),
                        ag[c][1, blocks].reshape(some * HEIGHT, COLS),
                    ],
                    axis=1,
                )
                v = jnp.dot(a, w, preferred_element_type=jnp.float32)
                v = v.reshape(some, HEIGHT, v.shape[1])
                if col > 0:
                    v = v + total[blocks]
                if col < COL_CHUNKS - 1:
                    total[blocks] = v
                else:
                    v = jnp.maximum(v + bias[...][None], 0.0)
                    out[blocks, row * HEIGHT : (row + 1) * HEIGHT, :] = v.astype(out.dtype)
                return carry

            lax.fori_loop(0, LB // some, mixing, 0)

    for c in range(CHUNKS):
        for copies, hops in ring.values():
            for k in range(hops):
                for item in copies(c, k):
                    item.wait_send()
        h_copy(c).wait_send()
    for item in along_z + along_x + along_y:
        item.wait_send()


def vmem():
    return pl.BlockSpec(memory_space=pltpu.VMEM)


def smem():
    return pl.BlockSpec(memory_space=pltpu.SMEM)


def local(
    source_feats, rel_weight, tiles, src_blk, rel_id, owner, local_blk, in_degree, mix_weight, bias
):
    n_rows = lax.axis_size("rows")
    src_dev, half_w = source_feats.shape
    tile = tiles.shape[1]
    parts, per_row = src_blk.shape
    n_rel = rel_weight.shape[0]
    n_src_blocks = src_dev // tile
    n_local = in_degree.shape[0] // tile

    me = lax.axis_index("rows")
    spot_z = lax.broadcasted_iota(jnp.int32, (NZ, 128), 0) == me // (NX * NY)
    spot_x = lax.broadcasted_iota(jnp.int32, (NZ, 128), 1) // LB == (me // NY) % NX
    own = jnp.tile(owner[:, 0] * LB + local_blk, 128 // parts)
    key = jnp.where(spot_z & spot_x, own[None, :], 0)
    weight = rel_weight.reshape(n_rel, half_w, half_w)
    n_hops = NZ + NX + NY - 3
    degree = in_degree.astype(jnp.float32)
    block = lambda n: [pltpu.VMEM((n, HEIGHT, COLS), jnp.bfloat16)] * CHUNKS
    dma = pltpu.SemaphoreType.DMA
    pair = lambda n: [dma((CHUNKS, n, 2)), dma((CHUNKS, n, 2))]
    out, flag = pl.pallas_call(
        functools.partial(layer_kernel, schedule()),
        out_shape=(
            jax.ShapeDtypeStruct((n_local, tile, half_w), jnp.bfloat16),
            jax.ShapeDtypeStruct((1, 1), jnp.int32),
        ),
        in_specs=[smem(), smem()] + [vmem()] * 7,
        out_specs=(vmem(), smem()),
        scratch_shapes=[
            pltpu.VMEM((n_rel * n_src_blocks, tile, half_w), jnp.bfloat16),
            pltpu.VMEM((CHUNKS, parts, HEIGHT, COLS), jnp.bfloat16),
            pltpu.VMEM((NY, NX, NZ, 8, 128), jnp.int32),
            pltpu.VMEM((8, 128), jnp.int32),
            pltpu.SMEM((8, 128), jnp.int32),
            pltpu.VMEM((8, 128), jnp.int32),
            pltpu.SMEM((8, 128), jnp.int32),
        ]
        + block(2 * Z_CAP[0])
        + block(Z_SLOTS)
        + block(2 * X_CAP[0])
        + block(X_SLOTS)
        + block(2 * Y_CAP[0])
        + block(Y_SLOTS)
        + block(2 * R_LIST)
        + block(2 * R_LIST + 2 * FAR + GROUP)
        + [pltpu.VMEM((2, n_local, HEIGHT, COLS), jnp.bfloat16)] * CHUNKS
        + [
            pltpu.VMEM((MERGE + 1, HEIGHT, COLS), jnp.bfloat16),
            pltpu.VMEM((n_local, HEIGHT, half_w), jnp.float32),
            pltpu.VMEM((n_local, tile, COLS), jnp.float32),
        ]
        + pair(len(Z_CAP))
        + pair(len(X_CAP))
        + pair(len(Y_CAP))
        + pair(2)
        + [dma((CHUNKS,)), dma((CHUNKS,)), dma((n_hops,)), dma((n_hops,)), dma((2,))],
        compiler_params=pltpu.CompilerParams(
            collective_id=0, has_side_effects=True, vmem_limit_bytes=67043328
        ),
    )(rel_id.T, src_blk.T, key, source_feats, weight, tiles, in_degree.reshape(-1, 128), mix_weight, bias[None, :])
    out = out.reshape(n_local * tile, half_w)

    def dense():
        partials = pl.pallas_call(
            partials_kernel,
            out_shape=jax.ShapeDtypeStruct((parts, tile, half_w), jnp.bfloat16),
            in_specs=[smem(), smem(), vmem(), vmem(), vmem()],
            out_specs=vmem(),
            scratch_shapes=[pltpu.VMEM((n_rel * n_src_blocks, tile, half_w), jnp.bfloat16)],
        )(rel_id.T, src_blk.T, source_feats, weight, tiles).reshape(parts, tile * half_w)
        capacity = max(2, 2 * parts // n_rows)
        target_dev = owner[:, 0]
        positions = jnp.arange(parts, dtype=jnp.int32)
        earlier = (target_dev[:, None] == target_dev[None, :]) & (
            positions[None, :] < positions[:, None]
        )
        rank = jnp.sum(earlier.astype(jnp.int32), axis=1)
        slot = target_dev * capacity + rank
        slot_ids = jnp.arange(n_rows * capacity, dtype=jnp.int32)
        placing = slot_ids[:, None] == slot[None, :]
        outgoing = jnp.dot(
            placing.astype(jnp.bfloat16), partials, preferred_element_type=jnp.float32
        ).astype(jnp.bfloat16)
        out_ids = jnp.sum(jnp.where(placing, local_blk[None, :] + 1, 0), axis=1) - 1
        block_index = jnp.arange(n_local, dtype=jnp.int32)
        arrived = lax.all_to_all(outgoing, "rows", split_axis=0, concat_axis=0, tiled=True)
        arrived_ids = lax.all_to_all(out_ids, "rows", split_axis=0, concat_axis=0, tiled=True)
        selector = (arrived_ids[None, :] == block_index[:, None]).astype(jnp.bfloat16)
        summed = jnp.dot(selector, arrived, preferred_element_type=jnp.float32)
        summed = summed.reshape(n_local * tile, half_w)
        agg = (summed / degree[:, None]).astype(jnp.bfloat16)
        theirs = lax.ppermute(agg, "half", [(0, 1), (1, 0)])
        half = lax.axis_index("half")
        w_mine = lax.dynamic_slice_in_dim(mix_weight, half * half_w, half_w, 0)
        w_theirs = lax.dynamic_slice_in_dim(mix_weight, (1 - half) * half_w, half_w, 0)
        mixed = jnp.dot(
            jnp.concatenate([agg, theirs], axis=1),
            jnp.concatenate([w_mine, w_theirs], axis=0),
            preferred_element_type=jnp.float32,
        )
        return jax.nn.relu(mixed + bias).astype(jnp.bfloat16)

    return lax.cond(flag[0, 0] > 0, dense, lambda: out)


def solution(mesh):
    placed = (
        P("rows", "half"),
        P(None, "half", None, None),
        P("rows", None, None),
        P("rows", None),
        P("rows", None),
        P("rows", None),
        P("rows"),
        P("rows"),
        P(None, "half"),
        P("half"),
    )
    return jax.shard_map(
        local, mesh=mesh, in_specs=placed, out_specs=P("rows", "half"), check_vma=False
    )
```
